256 devices in a mesh: shard: 8 (over y, core), tensor: 4 (over x), section: 8 (over z).
Axes of the slice: x: 4, y: 4, z: 8, core: 2. Of those that a mesh axis runs over, the one named last changes fastest.
Arguments:
- normed_inputs: bfloat16 [65536, 4096], P(('shard', 'section')), may hold values from -320 to 320
- projection_cotangent: bfloat16 [65536, 2, 1024], P(('shard', 'section'), None, 'tensor'), may hold values from -1 to 1
- small_partials: bfloat16 [64, 10, 4096], P(('shard', 'section'), None, 'tensor'), may hold values from -2000 to 2000
- master_weights: float32 [4096, 2, 1024], P(('shard', 'section'), None, 'tensor'), may hold values from -4 to 4
- first_moment: float32 [4096, 2, 1024], P(('shard', 'section'), None, 'tensor'), may hold values from -3 to 3
- second_moment: float32 [4096, 2, 1024], P(('shard', 'section'), None, 'tensor'), may hold values from 0.05 to 1
- small_master: float32 [10, 4096], P(None, 'tensor'), may hold values from -4 to 4
- small_first: float32 [10, 4096], P(None, 'tensor'), may hold values from -3 to 3
- small_second: float32 [10, 4096], P(None, 'tensor'), may hold values from 0.05 to 1
Outputs:
- updated_master: float32 [4096, 2, 1024], P(('shard', 'section'), None, 'tensor')
- updated_first: float32 [4096, 2, 1024], P(('shard', 'section'), None, 'tensor')
- updated_second: float32 [4096, 2, 1024], P(('shard', 'section'), None, 'tensor')
- gathered_weights: bfloat16 [4096, 2, 1024], P(None, None, 'tensor')
- small_updated_master: float32 [10, 4096], P(None, 'tensor')
- small_updated_first: float32 [10, 4096], P(None, 'tensor')
- small_updated_second: float32 [10, 4096], P(None, 'tensor')
- small_weights: bfloat16 [10, 4096], P(None, 'tensor')
The draws below stay inside these ranges and needn't reach their ends.
All inputs are finite; a program needn't handle non-finite values.
Results may differ from the reference program's by a relative error of at most 0.0015.
Values may be sent and summed in bfloat16 or wider, within the bound.
A program may use at most 64 MiB of HBM per device.

```python
import math
import jax
import jax.numpy as jnp
from jax import lax

D = 4096
EXPERTS = 8
STEP = 10
KV_COLS = 1024
SMALL_ROWS = 10
REPLICAS = 64
TOKENS = 65536


def rising_scales(key, length):
    rise = jnp.sqrt(1.0 + 2.0 * jnp.arange(length, dtype=jnp.float32) / length)
    return rise * jnp.exp(jax.random.uniform(key, (length,), minval=0.0, maxval=math.log(10.0)))


def base_values(key, shape):
    return jnp.clip(jax.random.normal(key, shape), -5.0, 5.0)


def draw_normed_inputs(key, part):
    first_key, second_key = jax.random.split(key, 2)
    features = rising_scales(second_key, D)
    values = base_values(first_key, (TOKENS, D)) * features[None, :]
    return values.astype(jnp.bfloat16)


def draw_projection_cotangent(key, part):
    first_key, second_key = jax.random.split(key, 2)
    columns = rising_scales(second_key, 2 * KV_COLS).reshape(2, KV_COLS)
    values = base_values(first_key, (TOKENS, 2, KV_COLS)) * columns[None, :, :] * float(TOKENS) ** (-0.5)
    return values.astype(jnp.bfloat16)


def draw_small_partials(key, part):
    first_key, second_key, third_key = jax.random.split(key, 3)
    columns = rising_scales(second_key, D)
    rows_scale = jnp.exp(jax.random.uniform(third_key, (SMALL_ROWS,), minval=0.0, maxval=math.log(10.0)))
    values = 2.0 * base_values(first_key, (REPLICAS, SMALL_ROWS, D)) * rows_scale[None, :, None] * columns[None, None, :]
    return values.astype(jnp.bfloat16)


def levels(rng, extent, cuts, smallest, largest):
    factor_of = 1.0
    for axis_at, blocks in cuts:
        heights = jax.random.uniform(jax.random.fold_in(jax.random.fold_in(rng, 6), axis_at), (blocks,), jnp.float32, smallest / len(cuts), largest / len(cuts))
        factor_of = factor_of * jnp.repeat(jnp.exp(heights), extent[axis_at] // blocks).reshape((-1,) + (1,) * (len(extent) - 1 - axis_at))
    return factor_of


def noise(own_key, extent, width, most, cuts=(), held_as=jnp.bfloat16):
    gain = levels(own_key, extent, cuts, -0.22, 0.18) if cuts else 1.0
    drawn = jax.random.normal(own_key, extent, jnp.float32) * width * gain
    return jnp.minimum(jnp.maximum(drawn, -most), most).astype(held_as)


def setup_inputs(seed: int = 0) -> dict:
    seeds = jax.random.split(jax.random.key(seed), 10)
    normed_inputs = draw_normed_inputs(jax.random.fold_in(seeds[9], 71), 0)
    projection_cotangent = draw_projection_cotangent(jax.random.fold_in(seeds[9], 71), 0)
    small_partials = draw_small_partials(jax.random.fold_in(seeds[9], 71), 0)
    master_weights = noise(seeds[3], (D, 2, KV_COLS), 1.0, 4.0, ((0, 64), (2, 4)), jnp.float32)
    first_moment = noise(seeds[4], (D, 2, KV_COLS), 0.5, 3.0, ((0, 64), (2, 4)), jnp.float32)
    second_moment = jnp.clip(jnp.exp(math.log(1.0) - 2.9957323 * jax.random.uniform(seeds[5], (D, 2, KV_COLS), jnp.float32) ** levels(seeds[5], (D, 2, KV_COLS), ((0, 64), (2, 4)), -0.2, 0.2)), 0.05, 1.0)
    small_master = noise(seeds[6], (SMALL_ROWS, D), 1.0, 4.0, ((1, 4),), jnp.float32)
    small_first = noise(seeds[7], (SMALL_ROWS, D), 0.5, 3.0, ((1, 4),), jnp.float32)
    small_second = jnp.clip(jnp.exp(math.log(1.0) - 2.9957323 * jax.random.uniform(seeds[8], (SMALL_ROWS, D), jnp.float32) ** levels(seeds[8], (SMALL_ROWS, D), ((1, 4),), -0.2, 0.2)), 0.05, 1.0)
    return dict(normed_inputs=normed_inputs, projection_cotangent=projection_cotangent, small_partials=small_partials, master_weights=master_weights, first_moment=first_moment, second_moment=second_moment, small_master=small_master, small_first=small_first, small_second=small_second)


beta_one = 0.9
beta_two = 0.95
learning_rate = 0.01
weight_decay = 0.1
epsilon = 1e-08
clip_factor = 0.5

def adamw(gradient, scale, first, second, master, decay):
    clipped = gradient * scale
    first_new = beta_one * first + (1.0 - beta_one) * clipped
    second_new = beta_two * second + (1.0 - beta_two) * clipped * clipped
    first_hat = first_new / (1.0 - beta_one ** STEP)
    second_hat = second_new / (1.0 - beta_two ** STEP)
    master_new = master - learning_rate * (first_hat / (jnp.sqrt(second_hat) + epsilon) + decay * master)
    return (master_new, first_new, second_new)

def reference(normed_inputs, projection_cotangent, small_partials, master_weights, first_moment, second_moment, small_master, small_first, small_second):
    flat = projection_cotangent.reshape(TOKENS, 2 * KV_COLS)
    gradient = lax.dot_general(normed_inputs, flat, (((0,), (0,)), ((), ())), preferred_element_type=jnp.float32)
    gradient = gradient.reshape(D, 2, KV_COLS)
    small_gradient = lax.optimization_barrier(jnp.sum(small_partials.astype(jnp.float32), axis=0))
    total = jnp.sum(gradient * gradient) + jnp.sum(small_gradient * small_gradient)
    limit = clip_factor * math.sqrt(2 * D * KV_COLS + SMALL_ROWS * D)
    scale = jnp.minimum(1.0, limit / (jnp.sqrt(total) + 1e-06))
    master_new, first_new, second_new = adamw(gradient, scale, first_moment, second_moment, master_weights, weight_decay)
    row_decay = jnp.where(jnp.arange(SMALL_ROWS)[:, None] < EXPERTS, weight_decay, 0.0).astype(jnp.float32)
    small_master_new, small_first_new, small_second_new = adamw(small_gradient, scale, small_first, small_second, small_master, row_decay)
    return (master_new, first_new, second_new, master_new.astype(jnp.bfloat16), small_master_new, small_first_new, small_second_new, small_master_new.astype(jnp.bfloat16))
```

```python
import functools
import math

import jax
import jax.numpy as jnp
from jax import lax
from jax.experimental import pallas as pl
from jax.experimental.pallas import tpu as pltpu
from jax.sharding import PartitionSpec as P

D = 4096
EXPERTS = 8
STEP = 10
KV_COLS = 1024
SMALL_ROWS = 10

beta_one = 0.9
beta_two = 0.95
learning_rate = 0.01
weight_decay = 0.1
epsilon = 1e-08
clip_factor = 0.5

F32 = jnp.float32
BF16 = jnp.bfloat16
MESH = pl.DeviceIdType.MESH

ROWS = 64
HALF = 256
Z_FIRST = 16
LAST_Z = 96


def adamw(gradient, scale, first, second, master, decay):
    clipped = gradient * scale
    first_new = beta_one * first + (1.0 - beta_one) * clipped
    second_new = beta_two * second + (1.0 - beta_two) * clipped * clipped
    first_hat = first_new / (1.0 - beta_one**STEP)
    second_hat = second_new / (1.0 - beta_two**STEP)
    master_new = master - learning_rate * (
        first_hat / (jnp.sqrt(second_hat) + epsilon) + decay * master
    )
    return (master_new, first_new, second_new)


def folded(square):
    return square.reshape(-1, 8, 128).sum(axis=0)


def kernel(
    ny, nx, nz,
    g, small, mw, m1, m2, sm, s1, s2,
    om, o1, o2, gat, osm, os1, os2, osw,
    pair, za, yb, ra, rb, sy, ry, sz, szf, rz, own_grad,
    smz, smr, smc, smy, smf, nzs, ncs, nys, nxs,
    pair_s, pair_r, za_s, za_r, yb_s, yb_r, sy_s, sy_r, sz_s, sz_r,
    smz_s, smz_r, smc_s, smc_r, smy_s, smy_r, smf_s, smf_r,
    nz_s, nz_r, nc_s, nc_r, ny_s, ny_r, nx_s, nx_r,
    a1_s, a1_r, b1_s, b1_r, a2_s, a2_r, b2_s, b2_r, fa_s, fa_r, fb_s, fb_r,
):
    shard = lax.axis_index("shard")
    x = lax.axis_index("tensor")
    z = lax.axis_index("section")
    y, c = shard // 2, shard % 2
    other = 1 - c
    sibling = (y * 2 + other, x, z)

    def at_y(d):
        yy = (y + d) % ny
        return yy, (yy * 2 + c, x, z)

    def at_z(d):
        zz = (z + d) % nz
        return zz, (shard, x, zz)

    def at_x(d):
        xx = (x + d) % nx
        return xx, (shard, xx, z)

    def copy(src, dst, send, recv, device):
        return pltpu.make_async_remote_copy(
            src_ref=src, dst_ref=dst, send_sem=send, recv_sem=recv, device_id=device, device_id_type=MESH
        )

    sent = []

    def send(*a):
        made = copy(*a)
        made.start()
        sent.append(made)

    barrier = pltpu.get_barrier_semaphore()
    peers = [sibling] + [at_y(d)[1] for d in range(1, ny)] + [at_z(d)[1] for d in range(1, nz)] + [at_x(d)[1] for d in range(1, nx)]
    for peer in peers:
        pl.semaphore_signal(barrier, inc=1, device_id=peer, device_id_type=MESH)
    pl.semaphore_wait(barrier, len(peers))

    for d in list(range(1, ny)) + [0]:
        yy, _ = at_y(d)
        send(g.at[:, yy, other], pair.at[:, yy], pair_s.at[d], pair_r.at[yy], sibling)

    smz[...] = jnp.zeros_like(smz)
    for i in range(nz):
        smz[i, 0:SMALL_ROWS, :] = small[:, i * 128 : (i + 1) * 128].astype(F32)
    smr[z] = smz[z]
    for d in range(1, nz):
        zz, peer = at_z(d)
        send(smz.at[zz], smr.at[z], smz_s.at[d], smz_r.at[z], peer)

    for d in list(range(1, ny)) + [0]:
        yy, peer = at_y(d)
        copy(g.at[:, yy, other], pair.at[:, yy], pair_s.at[d], pair_r.at[yy], sibling).wait_recv()

        def add(i, carry, yy=yy):
            j, zz = i // nz, i % nz
            both = (g[j, yy, c, zz].astype(F32) + pair[j, yy, zz].astype(F32)).astype(BF16)
            za[zz, j, yy] = both[0:Z_FIRST]
            yb[yy, j, zz] = both[Z_FIRST:ROWS]
            return carry

        lax.fori_loop(0, 2 * nz, add, 0)
        if d:
            send(yb.at[yy], rb.at[y], yb_s.at[d], yb_r.at[y], peer)
    for d in range(1, nz):
        zz, peer = at_z(d)
        send(za.at[zz], ra.at[z], za_s.at[d], za_r.at[z], peer)

    for d in range(1, nz):
        zz, peer = at_z(d)
        copy(smz.at[zz], smr.at[zz], smz_s.at[d], smz_r.at[zz], peer).wait_recv()
    block = smr[0]
    for i in range(1, nz):
        block = block + smr[i]
    smc[c] = block
    send(smc.at[c], smc.at[c], smc_s.at[0], smc_r.at[c], sibling)

    for d in range(1, nz):
        zz, peer = at_z(d)
        copy(za.at[zz], ra.at[zz], za_s.at[d], za_r.at[zz], peer).wait_recv()

    def sum_z(i, carry):
        j, yy = i // ny, i % ny
        total = g[j, yy, c, z, 0:Z_FIRST].astype(F32) + pair[j, yy, z, 0:Z_FIRST].astype(F32)
        for d in range(1, nz):
            total = total + ra[(z + d) % nz, j, yy].astype(F32)
        sy[yy, j] = total
        return carry

    lax.fori_loop(0, 2 * ny, sum_z, 0)
    for d in range(1, ny):
        yy, peer = at_y(d)
        send(sy.at[yy], ry.at[y], sy_s.at[d], sy_r.at[y], peer)

    copy(smc.at[c], smc.at[other], smc_s.at[0], smc_r.at[other], sibling).wait_recv()
    smy[y] = smc[0] + smc[1]
    for d in range(1, ny):
        yy, peer = at_y(d)
        send(smy.at[y], smy.at[y], smy_s.at[d], smy_r.at[y], peer)

    for d in range(1, ny):
        yy, peer = at_y(d)
        copy(yb.at[yy], rb.at[yy], yb_s.at[d], yb_r.at[yy], peer).wait_recv()

    def sum_y(i, carry):
        j, zz = i // nz, i % nz
        total = g[j, y, c, zz, Z_FIRST:ROWS].astype(F32) + pair[j, y, zz, Z_FIRST:ROWS].astype(F32)
        for d in range(1, ny):
            total = total + rb[(y + d) % ny, j, zz].astype(F32)
        szf[zz, j] = total
        sz[zz, j] = total.astype(BF16)
        return carry

    lax.fori_loop(0, 2 * nz, sum_y, 0)
    for d in range(1, nz):
        zz, peer = at_z(d)
        send(sz.at[zz], rz.at[z], sz_s.at[d], sz_r.at[z], peer)

    for d in range(1, ny):
        yy, peer = at_y(d)
        copy(smy.at[y], smy.at[yy], smy_s.at[d], smy_r.at[yy], peer).wait_recv()
    block = smy[0]
    for i in range(1, ny):
        block = block + smy[i]
    smf[z] = block
    for d in range(1, nz):
        zz, peer = at_z(d)
        send(smf.at[z], smf.at[z], smf_s.at[d], smf_r.at[z], peer)

    for d in range(1, ny):
        yy, peer = at_y(d)
        copy(sy.at[yy], ry.at[yy], sy_s.at[d], sy_r.at[yy], peer).wait_recv()
    for j in range(2):
        total = sy[y, j]
        for d in range(1, ny):
            total = total + ry[(y + d) % ny, j]
        for q in range(2):
            own_grad[pl.ds(2 * q + j, Z_FIRST, stride=4), :] = total[:, q * 128 : (q + 1) * 128]
    for d in range(1, nz):
        zz, peer = at_z(d)
        copy(sz.at[zz], rz.at[zz], sz_s.at[d], sz_r.at[zz], peer).wait_recv()
    for j in range(2):
        total = szf[z, j]
        for d in range(1, nz):
            total = total + rz[(z + d) % nz, j].astype(F32)
        for q in range(2):
            own_grad[pl.ds(4 * Z_FIRST + 2 * q + j, ROWS - Z_FIRST, stride=4), :] = total[:, q * 128 : (q + 1) * 128]

    grad = own_grad[...]
    nzs[z] = folded(grad * grad)
    for d in range(1, nz):
        zz, peer = at_z(d)
        send(nzs.at[z], nzs.at[z], nz_s.at[d], nz_r.at[z], peer)
    for d in range(1, nz):
        zz, peer = at_z(d)
        copy(smf.at[z], smf.at[zz], smf_s.at[d], smf_r.at[zz], peer).wait_recv()
    small_square = jnp.zeros((8, 128), F32)
    for i in range(nz):
        rows = smf[i]
        small_square = small_square + folded(rows * rows)
    for d in range(1, nz):
        zz, peer = at_z(d)
        copy(nzs.at[z], nzs.at[zz], nz_s.at[d], nz_r.at[zz], peer).wait_recv()
    part = nzs[0]
    for i in range(1, nz):
        part = part + nzs[i]
    ncs[c] = part
    send(ncs.at[c], ncs.at[c], nc_s.at[0], nc_r.at[c], sibling)
    copy(ncs.at[c], ncs.at[other], nc_s.at[0], nc_r.at[other], sibling).wait_recv()
    nys[y] = ncs[0] + ncs[1]
    for d in range(1, ny):
        yy, peer = at_y(d)
        send(nys.at[y], nys.at[y], ny_s.at[d], ny_r.at[y], peer)
    for d in range(1, ny):
        yy, peer = at_y(d)
        copy(nys.at[y], nys.at[yy], ny_s.at[d], ny_r.at[yy], peer).wait_recv()
    part = small_square
    for i in range(ny):
        part = part + nys[i]
    nxs[x] = part
    for d in range(1, nx):
        xx, peer = at_x(d)
        send(nxs.at[x], nxs.at[x], nx_s.at[d], nx_r.at[x], peer)
    for d in range(1, nx):
        xx, peer = at_x(d)
        copy(nxs.at[x], nxs.at[xx], nx_s.at[d], nx_r.at[xx], peer).wait_recv()
    part = nxs[0]
    for i in range(1, nx):
        part = part + nxs[i]
    total = jnp.sum(part, keepdims=True)
    limit = clip_factor * math.sqrt(2 * D * KV_COLS + SMALL_ROWS * D)
    scale = jnp.minimum(1.0, limit / (jnp.sqrt(total) + 1e-06))

    master_new, first_new, second_new = adamw(grad, scale, m1[...], m2[...], mw[...], weight_decay)
    gat[y, c, z] = master_new.astype(BF16)

    for d in range(1, nz):
        zz, peer = at_z(d)
        part = gat.at[y, c, z, LAST_Z:256]
        send(part, part, b1_s.at[d], b1_r.at[z], peer)
    for d in range(1, ny):
        yy, peer = at_y(d)
        part = gat.at[y, c, z, 0:LAST_Z]
        send(part, part, a1_s.at[d], a1_r.at[y], peer)

    om[...] = master_new
    o1[...] = first_new
    o2[...] = second_new
    decay = jnp.where(lax.broadcasted_iota(jnp.int32, (SMALL_ROWS, 128), 0) < EXPERTS, weight_decay, 0.0).astype(F32)
    for i in range(nz):
        lanes = slice(i * 128, (i + 1) * 128)
        made = adamw(smf[i, 0:SMALL_ROWS, :], scale, s1[:, lanes], s2[:, lanes], sm[:, lanes], decay)
        osm[:, lanes], os1[:, lanes], os2[:, lanes] = made
        osw[:, lanes] = made[0].astype(BF16)

    def z_block(core, zz):
        return gat.at[:, core, zz, 0:LAST_Z]

    def y_block(core, yy):
        return gat.at[yy, core, :, LAST_Z:256]

    for d in range(1, ny):
        yy, peer = at_y(d)
        part = gat.at[yy, c, z, 0:LAST_Z]
        copy(part, part, a1_s.at[d], a1_r.at[yy], peer).wait_recv()
    for d in range(1, nz):
        zz, peer = at_z(d)
        send(z_block(c, z), z_block(c, z), a2_s.at[d], a2_r.at[z], peer)
    send(z_block(c, z), z_block(c, z), fa_s.at[0], fa_r.at[z], sibling)
    for d in range(1, nz):
        zz, peer = at_z(d)
        part = gat.at[y, c, zz, LAST_Z:256]
        copy(part, part, b1_s.at[d], b1_r.at[zz], peer).wait_recv()
    for d in range(1, ny):
        yy, peer = at_y(d)
        send(y_block(c, y), y_block(c, y), b2_s.at[d], b2_r.at[y], peer)
    send(y_block(c, y), y_block(c, y), fb_s.at[0], fb_r.at[y], sibling)

    def on_z(d):
        zz, peer = at_z(d)
        copy(z_block(c, zz), z_block(c, zz), a2_s.at[d], a2_r.at[zz], peer).wait_recv()
        send(z_block(c, zz), z_block(c, zz), fa_s.at[d], fa_r.at[zz], sibling)

    def on_y(d):
        yy, peer = at_y(d)
        copy(y_block(c, yy), y_block(c, yy), b2_s.at[d], b2_r.at[yy], peer).wait_recv()
        send(y_block(c, yy), y_block(c, yy), fb_s.at[d], fb_r.at[yy], sibling)

    near = sorted(range(1, nz), key=lambda d: min(d, nz - d))
    near_y = sorted(range(1, ny), key=lambda d: min(d, ny - d))
    for d in near:
        on_z(d)
        if near_y:
            on_y(near_y.pop(0))
    for d in range(nz):
        zz, _ = at_z(d)
        copy(z_block(c, zz), z_block(other, zz), fa_s.at[d], fa_r.at[zz], sibling).wait_recv()
    for d in range(ny):
        yy, _ = at_y(d)
        copy(y_block(c, yy), y_block(other, yy), fb_s.at[d], fb_r.at[yy], sibling).wait_recv()
    for made in sent:
        made.wait_send()


def stored(array):
    rows = array.shape[0]
    return array.reshape(rows, 2, 2, 128).transpose(0, 2, 1, 3).reshape(rows * 4, 128)


def unstored(array):
    rows = array.shape[0] // 4
    return array.reshape(rows, 2, 2, 128).transpose(0, 2, 1, 3).reshape(rows, 2, 256)


def body(
    ny, nx, nz,
    normed_inputs,
    projection_cotangent,
    small_partials,
    master_weights,
    first_moment,
    second_moment,
    small_master,
    small_first,
    small_second,
):
    gradient = jnp.einsum(
        "tf,tjc->fjc", normed_inputs, projection_cotangent, preferred_element_type=F32
    ).astype(BF16).transpose(1, 0, 2)
    features = gradient.shape[1]
    assert features == ny * 2 * nz * ROWS
    gradient = gradient.reshape(2, ny, 2, nz, ROWS, HALF)
    small_shape = jax.ShapeDtypeStruct(small_master.shape, F32)
    owned = jax.ShapeDtypeStruct((4 * ROWS, 128), F32)
    dma = pltpu.SemaphoreType.DMA
    vm = pltpu.VMEM
    last = ROWS - Z_FIRST
    along_y, along_z, along_x = [dma((ny,))] * 2, [dma((nz,))] * 2, [dma((nx,))] * 2
    pairs = [dma((2,))] * 2
    outs = pl.pallas_call(
        functools.partial(kernel, ny, nx, nz),
        out_shape=(
            owned, owned, owned,
            jax.ShapeDtypeStruct((ny, 2, nz, 4 * ROWS, 128), BF16),
            small_shape, small_shape, small_shape,
            jax.ShapeDtypeStruct(small_master.shape, BF16),
        ),
        in_specs=[pl.BlockSpec(memory_space=pltpu.VMEM)] * 8,
        out_specs=[pl.BlockSpec(memory_space=pltpu.VMEM)] * 8,
        scratch_shapes=[
            vm((2, ny, nz, ROWS, HALF), BF16),
            vm((nz, 2, ny, Z_FIRST, HALF), BF16),
            vm((ny, 2, nz, last, HALF), BF16),
            vm((nz, 2, ny, Z_FIRST, HALF), BF16),
            vm((ny, 2, nz, last, HALF), BF16),
            vm((ny, 2, Z_FIRST, HALF), F32),
            vm((ny, 2, Z_FIRST, HALF), F32),
            vm((nz, 2, last, HALF), BF16),
            vm((nz, 2, last, HALF), F32),
            vm((nz, 2, last, HALF), BF16),
            vm((4 * ROWS, 128), F32),
            vm((nz, 16, 128), F32),
            vm((nz, 16, 128), F32),
            vm((2, 16, 128), F32),
            vm((ny, 16, 128), F32),
            vm((nz, 16, 128), F32),
            vm((nz, 8, 128), F32),
            vm((2, 8, 128), F32),
            vm((ny, 8, 128), F32),
            vm((nx, 8, 128), F32),
            *along_y, *along_z, *along_y, *along_y, *along_z,
            *along_z, *pairs, *along_y, *along_z,
            *along_z, *pairs, *along_y, *along_x,
            *along_y, *along_z, *along_z, *along_y, *along_z, *along_y,
        ],
        compiler_params=pltpu.CompilerParams(
            collective_id=0, has_side_effects=True, vmem_limit_bytes=48 << 20
        ),
    )(
        gradient, small_partials[0], stored(master_weights), stored(first_moment), stored(second_moment),
        small_master, small_first, small_second,
    )
    return (
        unstored(outs[0]), unstored(outs[1]), unstored(outs[2]),
        unstored(outs[3].reshape(-1, 128)),
        outs[4], outs[5], outs[6], outs[7],
    )


def solution(mesh):
    ny, nx, nz = mesh.shape["shard"] // 2, mesh.shape["tensor"], mesh.shape["section"]
    rows = P(("shard", "section"), None, "tensor")
    flat = P(None, "tensor")
    return jax.shard_map(
        functools.partial(body, ny, nx, nz),
        mesh=mesh,
        in_specs=(P(("shard", "section"), None), rows, rows, rows, rows, rows, flat, flat, flat),
        out_specs=(rows, rows, rows, P(None, None, "tensor"), flat, flat, flat, flat),
        check_vma=False,
    )
```

```python
import functools
import math

import jax
import jax.numpy as jnp
from jax import lax
from jax.experimental import pallas as pl
from jax.experimental.pallas import tpu as pltpu
from jax.sharding import PartitionSpec as P

D = 4096
EXPERTS = 8
STEP = 10
KV_COLS = 1024
SMALL_ROWS = 10

beta_one = 0.9
beta_two = 0.95
learning_rate = 0.01
weight_decay = 0.1
epsilon = 1e-08
clip_factor = 0.5

F32 = jnp.float32
BF16 = jnp.bfloat16
MESH = pl.DeviceIdType.MESH

ROWS = 64
HALF = 256
Z_FIRST = 32
LAST_Z = 128


def adamw(gradient, scale, first, second, master, decay):
    clipped = gradient * scale
    first_new = beta_one * first + (1.0 - beta_one) * clipped
    second_new = beta_two * second + (1.0 - beta_two) * clipped * clipped
    first_hat = first_new / (1.0 - beta_one**STEP)
    second_hat = second_new / (1.0 - beta_two**STEP)
    master_new = master - learning_rate * (
        first_hat / (jnp.sqrt(second_hat) + epsilon) + decay * master
    )
    return (master_new, first_new, second_new)


def folded(square):
    return square.reshape(-1, 8, 128).sum(axis=0)


def kernel(
    ny, nx, nz,
    g, small, mw, m1, m2, sm, s1, s2,
    om, o1, o2, gat, osm, os1, os2, osw,
    pair, zc, zr, yb, rb, sy, ry, sz, szf, rz, own_grad,
    smz, smr, smc, smy, smf, nzc, nyx,
    pair_s, pair_r, zc_s, zc_r, yb_s, yb_r, sy_s, sy_r, sz_s, sz_r,
    smz_s, smz_r, smc_s, smc_r, smy_s, smy_r, smf_s, smf_r,
    nzc_s, nzc_r, nyx_s, nyx_r,
    a1_s, a1_r, b1_s, b1_r, gc_s, gc_r, b2_s, b2_r, fa_s, fa_r, fb_s, fb_r,
):
    shard = lax.axis_index("shard")
    x = lax.axis_index("tensor")
    z = lax.axis_index("section")
    y, c = shard // 2, shard % 2
    other = 1 - c
    sibling = (y * 2 + other, x, z)

    def at_y(d):
        yy = (y + d) % ny
        return yy, (yy * 2 + c, x, z)

    def at_z(d):
        zz = (z + d) % nz
        return zz, (shard, x, zz)

    def at_zc(d):
        zz, cc = (z + d // 2) % nz, (c + d % 2) % 2
        return zz * 2 + cc, (y * 2 + cc, x, zz)

    def at_yx(d):
        yy, xx = (y + d // nx) % ny, (x + d % nx) % nx
        return yy * nx + xx, (yy * 2 + c, xx, z)

    def copy(src, dst, send, recv, device):
        return pltpu.make_async_remote_copy(
            src_ref=src, dst_ref=dst, send_sem=send, recv_sem=recv, device_id=device, device_id_type=MESH
        )

    sent = []

    def send(*a):
        made = copy(*a)
        made.start()
        sent.append(made)

    barrier = pltpu.get_barrier_semaphore()
    peers = [at_zc(d)[1] for d in range(1, 2 * nz)] + [at_yx(d)[1] for d in range(1, ny * nx)]
    for peer in peers:
        pl.semaphore_signal(barrier, inc=1, device_id=peer, device_id_type=MESH)
    pl.semaphore_wait(barrier, len(peers))

    for d in list(range(1, ny)) + [0]:
        yy, _ = at_y(d)
        send(g.at[:, yy, other], pair.at[:, yy], pair_s.at[d], pair_r.at[yy], sibling)

    smz[...] = jnp.zeros_like(smz)
    for i in range(nz):
        smz[i, 0:SMALL_ROWS, :] = small[:, i * 128 : (i + 1) * 128].astype(F32)
    smr[z] = smz[z]
    for d in range(1, nz):
        zz, peer = at_z(d)
        send(smz.at[zz], smr.at[z], smz_s.at[d], smz_r.at[z], peer)

    for d in list(range(1, ny)) + [0]:
        yy, peer = at_y(d)
        copy(g.at[:, yy, other], pair.at[:, yy], pair_s.at[d], pair_r.at[yy], sibling).wait_recv()

        def add(i, carry, yy=yy):
            j, zz = i // nz, i % nz
            rows = slice(Z_FIRST, ROWS)
            both = (g[j, yy, c, zz, rows].astype(F32) + pair[j, yy, zz, rows].astype(F32)).astype(BF16)
            yb[yy, j, zz] = both
            return carry

        lax.fori_loop(0, 2 * nz, add, 0)
        if d:
            send(yb.at[yy], rb.at[y], yb_s.at[d], yb_r.at[y], peer)
    def own_z(j, zz):
        rows = slice(0, Z_FIRST)
        return g[j, :, c, zz, rows].astype(F32) + pair[j, :, zz, rows].astype(F32)

    hops = {(j, way): nz // 2 - (j ^ way) for j in range(2) for way in range(2)}

    def step_z(j, way, k):
        sign = 1 if way == 0 else nz - 1
        if k:
            copy(zc.at[j, way, k - 1], zr.at[j, way, k - 1], zc_s.at[j, way, k - 1], zc_r.at[j, way, k - 1], at_z(sign)[1]).wait_recv()
        total = own_z(j, (z + sign * (hops[j, way] - k)) % nz)
        if k:
            total = total + zr[j, way, k - 1].astype(F32)
        zc[j, way, k] = total.astype(BF16)
        send(zc.at[j, way, k], zr.at[j, way, k], zc_s.at[j, way, k], zc_r.at[j, way, k], at_z(sign)[1])

    for j, way in hops:
        step_z(j, way, 0)
    for d in range(1, nz):
        zz, peer = at_z(d)
        copy(smz.at[zz], smr.at[zz], smz_s.at[d], smz_r.at[zz], peer).wait_recv()
    block = smr[0]
    for i in range(1, nz):
        block = block + smr[i]
    smc[c] = block
    send(smc.at[c], smc.at[c], smc_s.at[0], smc_r.at[c], sibling)

    for k in range(1, nz // 2):
        for j, way in hops:
            if k < hops[j, way]:
                step_z(j, way, k)
    for j in range(2):
        total = own_z(j, z)
        for way in range(2):
            k = hops[j, way] - 1
            peer = at_z(1 if way == 0 else nz - 1)[1]
            copy(zc.at[j, way, k], zr.at[j, way, k], zc_s.at[j, way, k], zc_r.at[j, way, k], peer).wait_recv()
            total = total + zr[j, way, k].astype(F32)
        sy[:, j] = total
    for d in range(1, ny):
        yy, peer = at_y(d)
        send(sy.at[yy], ry.at[y], sy_s.at[d], sy_r.at[y], peer)

    copy(smc.at[c], smc.at[other], smc_s.at[0], smc_r.at[other], sibling).wait_recv()
    smy[y] = smc[0] + smc[1]
    for d in range(1, ny):
        yy, peer = at_y(d)
        send(smy.at[y], smy.at[y], smy_s.at[d], smy_r.at[y], peer)

    for d in range(1, ny):
        yy, peer = at_y(d)
        copy(yb.at[yy], rb.at[yy], yb_s.at[d], yb_r.at[yy], peer).wait_recv()

    def sum_y(i, carry):
        j, zz = i // nz, i % nz
        total = g[j, y, c, zz, Z_FIRST:ROWS].astype(F32) + pair[j, y, zz, Z_FIRST:ROWS].astype(F32)
        for d in range(1, ny):
            total = total + rb[(y + d) % ny, j, zz].astype(F32)
        szf[zz, j] = total
        sz[zz, j] = total.astype(BF16)
        return carry

    lax.fori_loop(0, 2 * nz, sum_y, 0)
    for d in range(1, nz):
        zz, peer = at_z(d)
        send(sz.at[zz], rz.at[z], sz_s.at[d], sz_r.at[z], peer)

    for d in range(1, ny):
        yy, peer = at_y(d)
        copy(smy.at[y], smy.at[yy], smy_s.at[d], smy_r.at[yy], peer).wait_recv()
    block = smy[0]
    for i in range(1, ny):
        block = block + smy[i]
    smf[z] = block
    for d in range(1, nz):
        zz, peer = at_z(d)
        send(smf.at[z], smf.at[z], smf_s.at[d], smf_r.at[z], peer)

    for d in range(1, ny):
        yy, peer = at_y(d)
        copy(sy.at[yy], ry.at[yy], sy_s.at[d], sy_r.at[yy], peer).wait_recv()
    for j in range(2):
        total = sy[y, j]
        for d in range(1, ny):
            total = total + ry[(y + d) % ny, j]
        for q in range(2):
            own_grad[pl.ds(2 * q + j, Z_FIRST, stride=4), :] = total[:, q * 128 : (q + 1) * 128]
    for d in range(1, nz):
        zz, peer = at_z(d)
        copy(sz.at[zz], rz.at[zz], sz_s.at[d], sz_r.at[zz], peer).wait_recv()
    for j in range(2):
        total = szf[z, j]
        for d in range(1, nz):
            total = total + rz[(z + d) % nz, j].astype(F32)
        for q in range(2):
            own_grad[pl.ds(4 * Z_FIRST + 2 * q + j, ROWS - Z_FIRST, stride=4), :] = total[:, q * 128 : (q + 1) * 128]

    grad = own_grad[...]
    here = z * 2 + c
    nzc[here] = folded(grad * grad)
    for d in range(1, 2 * nz):
        there, peer = at_zc(d)
        send(nzc.at[here], nzc.at[here], nzc_s.at[d], nzc_r.at[here], peer)
    for d in range(1, nz):
        zz, peer = at_z(d)
        copy(smf.at[z], smf.at[zz], smf_s.at[d], smf_r.at[zz], peer).wait_recv()
    small_square = jnp.zeros((8, 128), F32)
    for i in range(nz):
        rows = smf[i]
        small_square = small_square + folded(rows * rows)
    for d in range(1, 2 * nz):
        there, peer = at_zc(d)
        copy(nzc.at[here], nzc.at[there], nzc_s.at[d], nzc_r.at[there], peer).wait_recv()
    part = small_square * (1.0 / ny)
    for i in range(2 * nz):
        part = part + nzc[i]
    here = y * nx + x
    nyx[here] = part
    for d in range(1, ny * nx):
        there, peer = at_yx(d)
        send(nyx.at[here], nyx.at[here], nyx_s.at[d], nyx_r.at[here], peer)
    for d in range(1, ny * nx):
        there, peer = at_yx(d)
        copy(nyx.at[here], nyx.at[there], nyx_s.at[d], nyx_r.at[there], peer).wait_recv()
    part = nyx[0]
    for i in range(1, ny * nx):
        part = part + nyx[i]
    total = jnp.sum(part, keepdims=True)
    limit = clip_factor * math.sqrt(2 * D * KV_COLS + SMALL_ROWS * D)
    scale = jnp.minimum(1.0, limit / (jnp.sqrt(total) + 1e-06))

    master_new, first_new, second_new = adamw(grad, scale, m1[...], m2[...], mw[...], weight_decay)
    gat[y, c, z] = master_new.astype(BF16)

    for d in range(1, nz):
        zz, peer = at_z(d)
        part = gat.at[y, c, z, LAST_Z:256]
        send(part, part, b1_s.at[d], b1_r.at[z], peer)
    for d in range(1, ny):
        yy, peer = at_y(d)
        part = gat.at[y, c, z, 0:LAST_Z]
        send(part, part, a1_s.at[d], a1_r.at[y], peer)

    om[...] = master_new
    o1[...] = first_new
    o2[...] = second_new
    decay = jnp.where(lax.broadcasted_iota(jnp.int32, (SMALL_ROWS, 128), 0) < EXPERTS, weight_decay, 0.0).astype(F32)
    for i in range(nz):
        lanes = slice(i * 128, (i + 1) * 128)
        made = adamw(smf[i, 0:SMALL_ROWS, :], scale, s1[:, lanes], s2[:, lanes], sm[:, lanes], decay)
        osm[:, lanes], os1[:, lanes], os2[:, lanes] = made
        osw[:, lanes] = made[0].astype(BF16)

    def z_block(core, zz, half):
        return gat.at[:, core, zz, half * (LAST_Z // 2) : (half + 1) * (LAST_Z // 2)]

    def y_block(core, yy):
        return gat.at[yy, core, :, LAST_Z:256]

    for d in range(1, ny):
        yy, peer = at_y(d)
        part = gat.at[yy, c, z, 0:LAST_Z]
        copy(part, part, a1_s.at[d], a1_r.at[yy], peer).wait_recv()

    def step_g(half, way, k):
        sign = 1 if way == 0 else nz - 1
        zz = (z + (nz - sign) * k) % nz
        part = z_block(c, zz, half)
        if k:
            copy(part, part, gc_s.at[half, way, k - 1], gc_r.at[half, way, k - 1], at_z(nz - sign)[1]).wait_recv()
        if k < hops[half, way]:
            send(part, part, gc_s.at[half, way, k], gc_r.at[half, way, k], at_z(sign)[1])
        if k or way == 0:
            send(part, part, fa_s.at[half, way, k], fa_r.at[half, way, k], sibling)

    for half, way in hops:
        step_g(half, way, 0)
    for d in range(1, nz):
        zz, peer = at_z(d)
        part = gat.at[y, c, zz, LAST_Z:256]
        copy(part, part, b1_s.at[d], b1_r.at[zz], peer).wait_recv()
    for d in range(1, ny):
        yy, peer = at_y(d)
        send(y_block(c, y), y_block(c, y), b2_s.at[d], b2_r.at[y], peer)
    send(y_block(c, y), y_block(c, y), fb_s.at[0], fb_r.at[y], sibling)

    def on_y(d):
        yy, peer = at_y(d)
        copy(y_block(c, yy), y_block(c, yy), b2_s.at[d], b2_r.at[yy], peer).wait_recv()
        send(y_block(c, yy), y_block(c, yy), fb_s.at[d], fb_r.at[yy], sibling)

    near_y = sorted(range(1, ny), key=lambda d: min(d, ny - d))
    for k in range(1, nz // 2 + 1):
        for half, way in hops:
            if k <= hops[half, way]:
                step_g(half, way, k)
        if k >= 2 and near_y:
            on_y(near_y.pop(0))
    for d in near_y:
        on_y(d)
    for half, way in hops:
        for k in range(way, hops[half, way] + 1):
            sign = 1 if way == 0 else nz - 1
            zz = (z + (nz - sign) * k) % nz
            copy(z_block(c, zz, half), z_block(other, zz, half), fa_s.at[half, way, k], fa_r.at[half, way, k], sibling).wait_recv()
    for d in range(ny):
        yy, _ = at_y(d)
        copy(y_block(c, yy), y_block(other, yy), fb_s.at[d], fb_r.at[yy], sibling).wait_recv()
    for made in sent:
        made.wait_send()


def leave(count, *refs):
    semaphores = refs[2 * count]
    copies = [pltpu.make_async_copy(refs[i], refs[count + i], semaphores.at[i]) for i in range(count)]
    for made in copies:
        made.start()
    for made in copies:
        made.wait()


def stored(array):
    rows = array.shape[0]
    return array.reshape(rows, 2, 2, 128).transpose(0, 2, 1, 3).reshape(rows * 4, 128)


def unstored(array):
    rows = array.shape[0] // 4
    return array.reshape(rows, 2, 2, 128).transpose(0, 2, 1, 3).reshape(rows, 2, 256)


def body(
    ny, nx, nz,
    normed_inputs,
    projection_cotangent,
    small_partials,
    master_weights,
    first_moment,
    second_moment,
    small_master,
    small_first,
    small_second,
):
    gradient = jnp.einsum(
        "tf,tjc->fjc", normed_inputs, projection_cotangent, preferred_element_type=F32
    ).astype(BF16).transpose(1, 0, 2)
    features = gradient.shape[1]
    assert features == ny * 2 * nz * ROWS
    gradient = gradient.reshape(2, ny, 2, nz, ROWS, HALF)
    small_shape = jax.ShapeDtypeStruct(small_master.shape, F32)
    owned = jax.ShapeDtypeStruct((4 * ROWS, 128), F32)
    dma = pltpu.SemaphoreType.DMA
    vm = pltpu.VMEM
    last = ROWS - Z_FIRST
    along_y, along_z = [dma((ny,))] * 2, [dma((nz,))] * 2
    pairs, chains = [dma((2,))] * 2, [dma((2, 2, nz // 2))] * 2
    outs = pl.pallas_call(
        functools.partial(kernel, ny, nx, nz),
        out_shape=(
            owned, owned, owned,
            jax.ShapeDtypeStruct((ny, 2, nz, 4 * ROWS, 128), BF16),
            small_shape, small_shape, small_shape,
            jax.ShapeDtypeStruct(small_master.shape, BF16),
        ),
        in_specs=[pl.BlockSpec(memory_space=pltpu.VMEM)] * 8,
        out_specs=[pl.BlockSpec(memory_space=pltpu.VMEM)] * 8,
        scratch_shapes=[
            vm((2, ny, nz, ROWS, HALF), BF16),
            vm((2, 2, nz // 2, ny, Z_FIRST, HALF), BF16),
            vm((2, 2, nz // 2, ny, Z_FIRST, HALF), BF16),
            vm((ny, 2, nz, last, HALF), BF16),
            vm((ny, 2, nz, last, HALF), BF16),
            vm((ny, 2, Z_FIRST, HALF), F32),
            vm((ny, 2, Z_FIRST, HALF), F32),
            vm((nz, 2, last, HALF), BF16),
            vm((nz, 2, last, HALF), F32),
            vm((nz, 2, last, HALF), BF16),
            vm((4 * ROWS, 128), F32),
            vm((nz, 16, 128), F32),
            vm((nz, 16, 128), F32),
            vm((2, 16, 128), F32),
            vm((ny, 16, 128), F32),
            vm((nz, 16, 128), F32),
            vm((2 * nz, 8, 128), F32),
            vm((ny * nx, 8, 128), F32),
            *along_y, *chains, *along_y, *along_y, *along_z,
            *along_z, *pairs, *along_y, *along_z,
            *[dma((2 * nz,))] * 2, *[dma((ny * nx,))] * 2,
            *along_y, *along_z, *chains, *along_y, *[dma((2, 2, nz // 2 + 1))] * 2, *along_y,
        ],
        compiler_params=pltpu.CompilerParams(
            collective_id=0, has_side_effects=True, vmem_limit_bytes=48 << 20
        ),
    )(
        gradient, small_partials[0], stored(master_weights), stored(first_moment), stored(second_moment),
        small_master, small_first, small_second,
    )
    count = len(outs)
    outs = pl.pallas_call(
        functools.partial(leave, count),
        out_shape=[jax.ShapeDtypeStruct(o.shape, o.dtype) for o in outs],
        in_specs=[pl.BlockSpec(memory_space=pltpu.VMEM)] * count,
        out_specs=[pl.BlockSpec(memory_space=pl.ANY)] * count,
        scratch_shapes=[dma((count,))],
        compiler_params=pltpu.CompilerParams(vmem_limit_bytes=16 << 20),
    )(*outs)
    return (
        unstored(outs[0]), unstored(outs[1]), unstored(outs[2]),
        unstored(outs[3].reshape(-1, 128)),
        outs[4], outs[5], outs[6], outs[7],
    )


def solution(mesh):
    ny, nx, nz = mesh.shape["shard"] // 2, mesh.shape["tensor"], mesh.shape["section"]
    rows = P(("shard", "section"), None, "tensor")
    flat = P(None, "tensor")
    return jax.shard_map(
        functools.partial(body, ny, nx, nz),
        mesh=mesh,
        in_specs=(P(("shard", "section"), None), rows, rows, rows, rows, rows, flat, flat, flat),
        out_specs=(rows, rows, rows, P(None, None, "tensor"), flat, flat, flat, flat),
        check_vma=False,
    )
```

```python
import functools
import math

import jax
import jax.numpy as jnp
from jax import lax
from jax.experimental import pallas as pl
from jax.experimental.pallas import tpu as pltpu
from jax.sharding import PartitionSpec as P

D = 4096
EXPERTS = 8
STEP = 10
KV_COLS = 1024
SMALL_ROWS = 10

beta_one = 0.9
beta_two = 0.95
learning_rate = 0.01
weight_decay = 0.1
epsilon = 1e-08
clip_factor = 0.5

F32 = jnp.float32
BF16 = jnp.bfloat16
MESH = pl.DeviceIdType.MESH

ROWS = 64
HALF = 256
Z_FIRST = 32
LAST_Z = 96


def adamw(gradient, scale, first, second, master, decay):
    clipped = gradient * scale
    first_new = beta_one * first + (1.0 - beta_one) * clipped
    second_new = beta_two * second + (1.0 - beta_two) * clipped * clipped
    first_hat = first_new / (1.0 - beta_one**STEP)
    second_hat = second_new / (1.0 - beta_two**STEP)
    master_new = master - learning_rate * (
        first_hat / (jnp.sqrt(second_hat) + epsilon) + decay * master
    )
    return (master_new, first_new, second_new)


def folded(square):
    return square.reshape(-1, 8, 128).sum(axis=0)


def kernel(
    ny, nx, nz,
    inputs, *refs,
):
    held = refs[:8]
    om, o1, o2, gat, osm, os1, os2, osw = refs[8:16]
    cotangent, small, mw, m1, m2, sm, s1, s2 = refs[16:24]
    (
        xv, wide, flat, gs, own, pair, zc, zr, yc, yr, sy, syf, ry, sz, szf, rz, own_grad,
        smz, smr, smc, smy, smf, nzc, nyx,
        in_s, x_s, pair_s, pair_r, zc_s, zc_r, yc_s, yc_r, sy_s, sy_r, sz_s, sz_r,
        smz_s, smz_r, smc_s, smc_r, smy_s, smy_r, smf_s, smf_r,
        nzc_s, nzc_r, nyx_s, nyx_r,
        a1_s, a1_r, b1_s, b1_r, gc_s, gc_r, b2_s, b2_r, b3_s, b3_r, fa_s, fa_r, fb_s, fb_r,
    ) = refs[24:]
    shard = lax.axis_index("shard")
    x = lax.axis_index("tensor")
    z = lax.axis_index("section")
    y, c = shard // 2, shard % 2
    other = 1 - c
    sibling = (y * 2 + other, x, z)

    def at_y(d):
        yy = (y + d) % ny
        return yy, (yy * 2 + c, x, z)

    def at_z(d):
        zz = (z + d) % nz
        return zz, (shard, x, zz)

    def at_zc(d):
        zz, cc = (z + d // 2) % nz, (c + d % 2) % 2
        return zz * 2 + cc, (y * 2 + cc, x, zz)

    def at_yx(d):
        yy, xx = (y + d // nx) % ny, (x + d % nx) % nx
        return yy * nx + xx, (yy * 2 + c, xx, z)

    def copy(src, dst, send, recv, device):
        return pltpu.make_async_remote_copy(
            src_ref=src, dst_ref=dst, send_sem=send, recv_sem=recv, device_id=device, device_id_type=MESH
        )

    sent = []

    def send(*a):
        made = copy(*a)
        made.start()
        sent.append(made)

    fills = [pltpu.make_async_copy(held[i], refs[16 + i], in_s.at[i]) for i in range(8)]
    fills[0].start()

    order = (2, 1, 3, 0)
    loads = {}
    for i, d in enumerate(order):
        for half, core in enumerate((other, c)):
            start = pl.multiple_of((at_y(d)[0] * 2 + core) * (nz * ROWS), nz * ROWS)
            slot = 2 * i + half
            loads[d, half] = slot, pltpu.make_async_copy(
                inputs.at[:, pl.ds(start, nz * ROWS)], xv.at[slot], x_s.at[slot]
            )
            loads[d, half][1].start()

    for fill in fills[1:]:
        fill.start()

    barrier = pltpu.get_barrier_semaphore()
    peers = [at_zc(d)[1] for d in range(1, 2 * nz)] + [at_yx(d)[1] for d in range(1, ny * nx)]
    for peer in peers:
        pl.semaphore_signal(barrier, inc=1, device_id=peer, device_id_type=MESH)

    tokens = flat.shape[0]
    fills[0].wait()
    wide[...] = cotangent[...].astype(F32)
    for j in range(2):
        for q in range(2):
            flat[:, j * HALF + q * 128 : j * HALF + (q + 1) * 128] = wide[
                pl.ds(2 * q + j, tokens, stride=4), :
            ].astype(BF16)

    def summed(d, half):
        slot, load = loads[d, half]
        load.wait()
        made = lax.dot_general(
            xv[slot], flat[...], (((0,), (0,)), ((), ())), preferred_element_type=F32
        )
        return made.reshape(nz, ROWS, 2 * HALF)

    def swap(d):
        yy, _ = at_y(d)
        return copy(gs.at[yy], pair.at[yy], pair_s.at[d], pair_r.at[yy], sibling)

    def other_half(d):
        gs[at_y(d)[0]] = summed(d, 0).astype(BF16)

    def own_half(d):
        own[at_y(d)[0]] = summed(d, 1)

    def start_swap(d):
        made = swap(d)
        made.start()
        sent.append(made)

    def columns(j):
        return slice(j * HALF, (j + 1) * HALF)

    def own_z(j, zz):
        rows = slice(0, Z_FIRST)
        return own[:, zz, rows, columns(j)] + pair[:, zz, rows, columns(j)].astype(F32)

    def own_y(j, yy):
        rows = slice(Z_FIRST, ROWS)
        return own[yy, :, rows, columns(j)] + pair[yy, :, rows, columns(j)].astype(F32)

    z_hops = {(j, way): nz // 2 - (j ^ way) for j in range(2) for way in range(2)}
    y_hops = {(j, way): ny // 2 - (j ^ way) for j in range(2) for way in range(2)}

    def chain(own_part, at, size, at_me, hops, buffers, sems, j, way, k):
        sign = 1 if way == 0 else size - 1
        out, arrived = buffers
        if k:
            copy(out.at[j, way, k - 1], arrived.at[j, way, k - 1], sems[0].at[j, way, k - 1], sems[1].at[j, way, k - 1], at(sign)[1]).wait_recv()
        if k == hops[j, way]:
            return arrived[j, way, k - 1].astype(F32)
        total = own_part(j, (at_me + sign * (hops[j, way] - k)) % size)
        if k:
            total = total + arrived[j, way, k - 1].astype(F32)
        out[j, way, k] = total.astype(BF16)
        send(out.at[j, way, k], arrived.at[j, way, k], sems[0].at[j, way, k], sems[1].at[j, way, k], at(sign)[1])

    step_z = functools.partial(chain, own_z, at_z, nz, z, z_hops, (zc, zr), (zc_s, zc_r))
    step_y = functools.partial(chain, own_y, at_y, ny, y, y_hops, (yc, yr), (yc_s, yc_r))

    other_half(2)
    pl.semaphore_wait(barrier, len(peers))
    start_swap(2)

    fills[1].wait()
    smz[...] = jnp.zeros_like(smz)
    for i in range(nz):
        smz[i, 0:SMALL_ROWS, :] = small[:, i * 128 : (i + 1) * 128].astype(F32)
    smr[z] = smz[z]
    for d in range(1, nz):
        zz, peer = at_z(d)
        send(smz.at[zz], smr.at[z], smz_s.at[d], smz_r.at[z], peer)

    own_half(2)
    other_half(1)
    start_swap(1)
    swap(2).wait_recv()
    step_y(0, 0, 0)
    step_y(1, 1, 0)
    own_half(1)
    other_half(3)
    start_swap(3)
    swap(1).wait_recv()
    step_y(1, 0, 0)
    own_half(3)
    other_half(0)
    start_swap(0)
    swap(3).wait_recv()
    step_y(0, 1, 0)
    own_half(0)
    swap(0).wait_recv()
    for j, way in z_hops:
        step_z(j, way, 0)
    step_y(0, 0, 1)
    step_y(1, 1, 1)

    for d in range(1, nz):
        zz, peer = at_z(d)
        copy(smz.at[zz], smr.at[zz], smz_s.at[d], smz_r.at[zz], peer).wait_recv()
    block = smr[0]
    for i in range(1, nz):
        block = block + smr[i]
    smc[c] = block
    send(smc.at[c], smc.at[c], smc_s.at[0], smc_r.at[c], sibling)

    def steps_z(k):
        for j, way in z_hops:
            if k < z_hops[j, way]:
                step_z(j, way, k)

    steps_z(1)
    copy(smc.at[c], smc.at[other], smc_s.at[0], smc_r.at[other], sibling).wait_recv()
    smy[y] = smc[0] + smc[1]
    for d in range(1, ny):
        yy, peer = at_y(d)
        send(smy.at[y], smy.at[y], smy_s.at[d], smy_r.at[y], peer)
    steps_z(2)

    for j in range(2):
        total = own_y(j, y)
        for way in range(2):
            total = total + step_y(j, way, y_hops[j, way])
        szf[:, :, columns(j)] = total
        sz[:, :, columns(j)] = total.astype(BF16)
    for d in range(1, nz):
        zz, peer = at_z(d)
        send(sz.at[zz], rz.at[z], sz_s.at[d], sz_r.at[z], peer)
    for k in range(3, nz // 2):
        steps_z(k)
    for d in range(1, ny):
        yy, peer = at_y(d)
        copy(smy.at[y], smy.at[yy], smy_s.at[d], smy_r.at[yy], peer).wait_recv()
    block = smy[0]
    for i in range(1, ny):
        block = block + smy[i]
    smf[z] = block
    for d in range(1, nz):
        zz, peer = at_z(d)
        send(smf.at[z], smf.at[z], smf_s.at[d], smf_r.at[z], peer)

    for j in range(2):
        total = own_z(j, z)
        for way in range(2):
            total = total + step_z(j, way, z_hops[j, way])
        syf[:, :, columns(j)] = total
        sy[:, :, columns(j)] = total.astype(BF16)
    for d in range(1, ny):
        yy, peer = at_y(d)
        send(sy.at[yy], ry.at[y], sy_s.at[d], sy_r.at[y], peer)

    def place(total, start):
        for j in range(2):
            for q in range(2):
                at = j * HALF + q * 128
                own_grad[pl.ds(4 * start + 2 * q + j, total.shape[0], stride=4), :] = total[:, at : at + 128]

    for d in range(1, nz):
        zz, peer = at_z(d)
        copy(sz.at[zz], rz.at[zz], sz_s.at[d], sz_r.at[zz], peer).wait_recv()
    total = szf[z]
    for d in range(1, nz):
        total = total + rz[(z + d) % nz].astype(F32)
    place(total, Z_FIRST)
    for d in range(1, nz):
        zz, peer = at_z(d)
        copy(smf.at[z], smf.at[zz], smf_s.at[d], smf_r.at[zz], peer).wait_recv()
    small_square = jnp.zeros((8, 128), F32)
    for i in range(nz):
        rows = smf[i]
        small_square = small_square + folded(rows * rows)
    for d in range(1, ny):
        yy, peer = at_y(d)
        copy(sy.at[yy], ry.at[yy], sy_s.at[d], sy_r.at[yy], peer).wait_recv()
    total = syf[y]
    for d in range(1, ny):
        total = total + ry[(y + d) % ny].astype(F32)
    place(total, 0)

    for fill in fills[2:]:
        fill.wait()
    grad = own_grad[...]
    here = z * 2 + c
    nzc[here] = folded(grad * grad)
    for d in range(1, 2 * nz):
        there, peer = at_zc(d)
        send(nzc.at[here], nzc.at[here], nzc_s.at[d], nzc_r.at[here], peer)
    for d in range(1, 2 * nz):
        there, peer = at_zc(d)
        copy(nzc.at[here], nzc.at[there], nzc_s.at[d], nzc_r.at[there], peer).wait_recv()
    part = small_square * (1.0 / ny)
    for i in range(2 * nz):
        part = part + nzc[i]
    here = y * nx + x
    nyx[here] = part
    for d in range(1, ny * nx):
        there, peer = at_yx(d)
        send(nyx.at[here], nyx.at[here], nyx_s.at[d], nyx_r.at[here], peer)
    for d in range(1, ny * nx):
        there, peer = at_yx(d)
        copy(nyx.at[here], nyx.at[there], nyx_s.at[d], nyx_r.at[there], peer).wait_recv()
    part = nyx[0]
    for i in range(1, ny * nx):
        part = part + nyx[i]
    total = jnp.sum(part, keepdims=True)
    limit = clip_factor * math.sqrt(2 * D * KV_COLS + SMALL_ROWS * D)
    scale = jnp.minimum(1.0, limit / (jnp.sqrt(total) + 1e-06))

    master_new, first_new, second_new = adamw(grad, scale, m1[...], m2[...], mw[...], weight_decay)
    gat[y, c, z] = master_new.astype(BF16)

    def z_block(core, zz, half):
        return gat.at[:, core, zz, half * (LAST_Z // 2) : (half + 1) * (LAST_Z // 2)]

    def piece(core, yy, zz):
        return gat.at[yy, core, zz, LAST_Z:256]

    def half_piece(core, yy, zz, way):
        middle = (LAST_Z + 256) // 2
        return gat.at[yy, core, zz, slice(LAST_Z, middle) if way == 0 else slice(middle, 256)]

    def on_both_y(zz):
        for way in range(2):
            part = piece(c, y, zz)
            send(part, part, b2_s.at[way, zz], b2_r.at[way, zz], at_y(1 if way == 0 else ny - 1)[1])
        send(piece(c, y, zz), piece(c, y, zz), fb_s.at[0, zz], fb_r.at[0, zz], sibling)

    def relay_y(zz):
        for way in range(2):
            sign = 1 if way == 0 else ny - 1
            behind, source = at_y(ny - sign)
            part = piece(c, behind, zz)
            copy(part, part, b2_s.at[way, zz], b2_r.at[way, zz], source).wait_recv()
            half = half_piece(c, behind, zz, way)
            send(half, half, b3_s.at[way, zz], b3_r.at[way, zz], at_y(sign)[1])
            send(part, part, fb_s.at[1 + way, zz], fb_r.at[1 + way, zz], sibling)

    def far_y(zz):
        across, source = at_y(ny // 2)
        for way in range(2):
            half = half_piece(c, across, zz, way)
            copy(half, half, b3_s.at[way, zz], b3_r.at[way, zz], source).wait_recv()
        send(piece(c, across, zz), piece(c, across, zz), fb_s.at[3, zz], fb_r.at[3, zz], sibling)

    b_hops = (nz // 2, nz // 2 - 1)

    def step_b(way, k):
        sign = 1 if way == 0 else nz - 1
        zz = (z + (nz - sign) * k) % nz
        part = piece(c, y, zz)
        if k:
            copy(part, part, b1_s.at[way, k - 1], b1_r.at[way, k - 1], at_z(nz - sign)[1]).wait_recv()
        if k < b_hops[way]:
            send(part, part, b1_s.at[way, k], b1_r.at[way, k], at_z(sign)[1])
        if k or way == 0:
            on_both_y(zz)

    def step_g(half, way, k):
        sign = 1 if way == 0 else nz - 1
        zz = (z + (nz - sign) * k) % nz
        part = z_block(c, zz, half)
        if k:
            copy(part, part, gc_s.at[half, way, k - 1], gc_r.at[half, way, k - 1], at_z(nz - sign)[1]).wait_recv()
        if k < z_hops[half, way]:
            send(part, part, gc_s.at[half, way, k], gc_r.at[half, way, k], at_z(sign)[1])
        if k or way == 0:
            send(part, part, fa_s.at[half, way, k], fa_r.at[half, way, k], sibling)

    def around(k):
        return [(z + (nz - k if way == 0 else k)) % nz for way in range(2) if k <= b_hops[way] and (k or way == 0)]

    step_b(0, 0)
    step_b(1, 0)
    for d in range(1, ny):
        yy, peer = at_y(d)
        part = gat.at[y, c, z, 0:LAST_Z]
        send(part, part, a1_s.at[d], a1_r.at[y], peer)

    om[...] = master_new
    o1[...] = first_new
    o2[...] = second_new

    for d in range(1, ny):
        yy, peer = at_y(d)
        part = gat.at[yy, c, z, 0:LAST_Z]
        copy(part, part, a1_s.at[d], a1_r.at[yy], peer).wait_recv()
    for half, way in z_hops:
        step_g(half, way, 0)
    for zz in around(0):
        relay_y(zz)

    decay = jnp.where(lax.broadcasted_iota(jnp.int32, (SMALL_ROWS, 128), 0) < EXPERTS, weight_decay, 0.0).astype(F32)
    for k in range(1, nz // 2 + 1):
        for way in range(2):
            if k <= b_hops[way]:
                step_b(way, k)
        for half, way in z_hops:
            if k <= z_hops[half, way]:
                step_g(half, way, k)
        for zz in around(k - 1):
            far_y(zz)
        for zz in around(k):
            relay_y(zz)
        if k == 1:
            for i in range(nz):
                lanes = slice(i * 128, (i + 1) * 128)
                made = adamw(smf[i, 0:SMALL_ROWS, :], scale, s1[:, lanes], s2[:, lanes], sm[:, lanes], decay)
                osm[:, lanes], os1[:, lanes], os2[:, lanes] = made
                osw[:, lanes] = made[0].astype(BF16)
    for zz in around(nz // 2):
        far_y(zz)

    for half, way in z_hops:
        for k in range(way, z_hops[half, way] + 1):
            zz = (z + (nz - k if way == 0 else k)) % nz
            copy(z_block(c, zz, half), z_block(other, zz, half), fa_s.at[half, way, k], fa_r.at[half, way, k], sibling).wait_recv()
    for i, d in enumerate((0, ny - 1, 1, ny // 2)):
        yy, _ = at_y(d)
        for zz in range(nz):
            copy(piece(c, yy, zz), piece(other, yy, zz), fb_s.at[i, zz], fb_r.at[i, zz], sibling).wait_recv()
    for made in sent:
        made.wait_send()


def leave(count, *refs):
    semaphores = refs[2 * count]
    copies = [pltpu.make_async_copy(refs[i], refs[count + i], semaphores.at[i]) for i in range(count)]
    for made in copies:
        made.start()
    for made in copies:
        made.wait()


def stored(array):
    rows = array.shape[0]
    return array.reshape(rows, 2, 2, 128).transpose(0, 2, 1, 3).reshape(rows * 4, 128)


def unstored(array):
    rows = array.shape[0] // 4
    return array.reshape(rows, 2, 2, 128).transpose(0, 2, 1, 3).reshape(rows, 2, 256)


def body(
    ny, nx, nz,
    normed_inputs,
    projection_cotangent,
    small_partials,
    master_weights,
    first_moment,
    second_moment,
    small_master,
    small_first,
    small_second,
):
    tokens, features = normed_inputs.shape
    assert ny == 4 and features == ny * 2 * nz * ROWS
    small_shape = jax.ShapeDtypeStruct(small_master.shape, F32)
    owned = jax.ShapeDtypeStruct((4 * ROWS, 128), F32)
    dma = pltpu.SemaphoreType.DMA
    vm = pltpu.VMEM
    last = ROWS - Z_FIRST
    along_y, along_z = [dma((ny,))] * 2, [dma((nz,))] * 2
    pairs, chains = [dma((2,))] * 2, [dma((2, 2, nz // 2))] * 2
    given = (
        normed_inputs, stored(projection_cotangent), small_partials[0],
        stored(master_weights), stored(first_moment), stored(second_moment),
        small_master, small_first, small_second,
    )
    given = [pltpu.with_memory_space_constraint(array, pltpu.HBM) for array in given]
    outs = pl.pallas_call(
        functools.partial(kernel, ny, nx, nz),
        out_shape=(
            owned, owned, owned,
            jax.ShapeDtypeStruct((ny, 2, nz, 4 * ROWS, 128), BF16),
            small_shape, small_shape, small_shape,
            jax.ShapeDtypeStruct(small_master.shape, BF16),
        ),
        in_specs=[pl.BlockSpec(memory_space=pltpu.HBM)] * 9,
        out_specs=[pl.BlockSpec(memory_space=pltpu.VMEM)] * 8,
        scratch_shapes=[
            *[vm(array.shape, array.dtype) for array in given[1:]],
            vm((2 * ny, tokens, nz * ROWS), BF16),
            vm((4 * tokens, 128), F32),
            vm((tokens, 2 * HALF), BF16),
            vm((ny, nz, ROWS, 2 * HALF), BF16),
            vm((ny, nz, ROWS, 2 * HALF), F32),
            vm((ny, nz, ROWS, 2 * HALF), BF16),
            *[vm((2, 2, nz // 2, ny, Z_FIRST, HALF), BF16)] * 2,
            *[vm((2, 2, ny // 2, nz, last, HALF), BF16)] * 2,
            vm((ny, Z_FIRST, 2 * HALF), BF16),
            vm((ny, Z_FIRST, 2 * HALF), F32),
            vm((ny, Z_FIRST, 2 * HALF), BF16),
            vm((nz, last, 2 * HALF), BF16),
            vm((nz, last, 2 * HALF), F32),
            vm((nz, last, 2 * HALF), BF16),
            vm((4 * ROWS, 128), F32),
            vm((nz, 16, 128), F32),
            vm((nz, 16, 128), F32),
            vm((2, 16, 128), F32),
            vm((ny, 16, 128), F32),
            vm((nz, 16, 128), F32),
            vm((2 * nz, 8, 128), F32),
            vm((ny * nx, 8, 128), F32),
            dma((8,)), dma((2 * ny,)), *along_y, *chains, *[dma((2, 2, ny // 2))] * 2, *along_y, *along_z,
            *along_z, *pairs, *along_y, *along_z,
            *[dma((2 * nz,))] * 2, *[dma((ny * nx,))] * 2,
            *along_y, *[dma((2, nz // 2))] * 2, *chains, *[dma((2, nz))] * 4, *[dma((2, 2, nz // 2 + 1))] * 2, *[dma((4, nz))] * 2,
        ],
        compiler_params=pltpu.CompilerParams(
            collective_id=0, has_side_effects=True, vmem_limit_bytes=36 << 20
        ),
    )(*given)
    count = len(outs)
    outs = pl.pallas_call(
        functools.partial(leave, count),
        out_shape=[jax.ShapeDtypeStruct(o.shape, o.dtype) for o in outs],
        in_specs=[pl.BlockSpec(memory_space=pltpu.VMEM)] * count,
        out_specs=[pl.BlockSpec(memory_space=pl.ANY)] * count,
        scratch_shapes=[dma((count,))],
        compiler_params=pltpu.CompilerParams(vmem_limit_bytes=16 << 20),
    )(*outs)
    return (
        unstored(outs[0]), unstored(outs[1]), unstored(outs[2]),
        unstored(outs[3].reshape(-1, 128)),
        outs[4], outs[5], outs[6], outs[7],
    )


def solution(mesh):
    ny, nx, nz = mesh.shape["shard"] // 2, mesh.shape["tensor"], mesh.shape["section"]
    rows = P(("shard", "section"), None, "tensor")
    flat = P(None, "tensor")
    return jax.shard_map(
        functools.partial(body, ny, nx, nz),
        mesh=mesh,
        in_specs=(P(("shard", "section"), None), rows, rows, rows, rows, rows, flat, flat, flat),
        out_specs=(rows, rows, rows, P(None, None, "tensor"), flat, flat, flat, flat),
        check_vma=False,
    )
```

```python
import functools
import math

import jax
import jax.numpy as jnp
from jax import lax
from jax.experimental import pallas as pl
from jax.experimental.pallas import tpu as pltpu
from jax.sharding import PartitionSpec as P

D = 4096
EXPERTS = 8
STEP = 10
KV_COLS = 1024
SMALL_ROWS = 10

beta_one = 0.9
beta_two = 0.95
learning_rate = 0.01
weight_decay = 0.1
epsilon = 1e-08
clip_factor = 0.5

F32 = jnp.float32
BF16 = jnp.bfloat16
MESH = pl.DeviceIdType.MESH

ROWS = 64
HALF = 256
Z_FIRST = 32
LAST_Z = 64


def adamw(gradient, scale, first, second, master, decay):
    clipped = gradient * scale
    first_new = beta_one * first + (1.0 - beta_one) * clipped
    second_new = beta_two * second + (1.0 - beta_two) * clipped * clipped
    first_hat = first_new / (1.0 - beta_one**STEP)
    second_hat = second_new / (1.0 - beta_two**STEP)
    master_new = master - learning_rate * (
        first_hat / (jnp.sqrt(second_hat) + epsilon) + decay * master
    )
    return (master_new, first_new, second_new)


def folded(square):
    return square.reshape(-1, 8, 128).sum(axis=0)


def kernel(
    ny, nx, nz,
    inputs, *refs,
):
    held = refs[:8]
    om, o1, o2, gat, osm, os1, os2, osw = refs[8:16]
    cotangent, small, mw, m1, m2, sm, s1, s2 = refs[16:24]
    (
        xv, wide, flat, gs, own, pair, zc, zr, yc, yr, sy, syf, ry, wc, wr, szf, own_grad,
        smz, smr, smc, smy, smf, nzc, nyx,
        in_s, x_s, pair_s, pair_r, zc_s, zc_r, yc_s, yc_r, sy_s, sy_r, wc_s, wc_r,
        smz_s, smz_r, smc_s, smc_r, smy_s, smy_r, smf_s, smf_r,
        nzc_s, nzc_r, nyx_s, nyx_r,
        a1_s, a1_r, b1_s, b1_r, gc_s, gc_r, b2_s, b2_r, b3_s, b3_r, fa_s, fa_r, fb_s, fb_r,
    ) = refs[24:]
    shard = lax.axis_index("shard")
    x = lax.axis_index("tensor")
    z = lax.axis_index("section")
    y, c = shard // 2, shard % 2
    other = 1 - c
    sibling = (y * 2 + other, x, z)

    def at_y(d):
        yy = (y + d) % ny
        return yy, (yy * 2 + c, x, z)

    def at_z(d):
        zz = (z + d) % nz
        return zz, (shard, x, zz)

    def at_zc(d):
        zz, cc = (z + d // 2) % nz, (c + d % 2) % 2
        return zz * 2 + cc, (y * 2 + cc, x, zz)

    def at_yx(d):
        yy, xx = (y + d // nx) % ny, (x + d % nx) % nx
        return yy * nx + xx, (yy * 2 + c, xx, z)

    def copy(src, dst, send, recv, device):
        return pltpu.make_async_remote_copy(
            src_ref=src, dst_ref=dst, send_sem=send, recv_sem=recv, device_id=device, device_id_type=MESH
        )

    sent = []

    def send(*a):
        made = copy(*a)
        made.start()
        sent.append(made)

    fills = [pltpu.make_async_copy(held[i], refs[16 + i], in_s.at[i]) for i in range(8)]
    fills[0].start()

    order = (2, 1, 3, 0)
    loads = {}
    for i, d in enumerate(order):
        for half, core in enumerate((other, c)):
            start = pl.multiple_of((at_y(d)[0] * 2 + core) * (nz * ROWS), nz * ROWS)
            slot = 2 * i + half
            loads[d, half] = slot, pltpu.make_async_copy(
                inputs.at[:, pl.ds(start, nz * ROWS)], xv.at[slot], x_s.at[slot]
            )
            loads[d, half][1].start()

    for fill in fills[1:]:
        fill.start()

    barrier = pltpu.get_barrier_semaphore()
    peers = [at_zc(d)[1] for d in range(1, 2 * nz)] + [at_yx(d)[1] for d in range(1, ny * nx)]
    for peer in peers:
        pl.semaphore_signal(barrier, inc=1, device_id=peer, device_id_type=MESH)

    tokens = flat.shape[0]
    fills[0].wait()
    wide[...] = cotangent[...].astype(F32)
    for j in range(2):
        for q in range(2):
            flat[:, j * HALF + q * 128 : j * HALF + (q + 1) * 128] = wide[
                pl.ds(2 * q + j, tokens, stride=4), :
            ].astype(BF16)

    def summed(d, half):
        slot, load = loads[d, half]
        load.wait()
        made = lax.dot_general(
            xv[slot], flat[...], (((0,), (0,)), ((), ())), preferred_element_type=F32
        )
        return made.reshape(nz, ROWS, 2 * HALF)

    def swap(d):
        yy, _ = at_y(d)
        return copy(gs.at[yy], pair.at[yy], pair_s.at[d], pair_r.at[yy], sibling)

    def other_half(d):
        gs[at_y(d)[0]] = summed(d, 0).astype(BF16)

    def own_half(d):
        own[at_y(d)[0]] = summed(d, 1)

    def start_swap(d):
        made = swap(d)
        made.start()
        sent.append(made)

    def columns(j):
        return slice(j * HALF, (j + 1) * HALF)

    def own_z(j, zz):
        rows = slice(0, Z_FIRST)
        return own[:, zz, rows, columns(j)] + pair[:, zz, rows, columns(j)].astype(F32)

    def own_y(j, yy):
        rows = slice(Z_FIRST, ROWS)
        return own[yy, :, rows, columns(j)] + pair[yy, :, rows, columns(j)].astype(F32)

    def own_w(j, zz):
        return szf[zz, :, columns(j)]

    z_hops = {(j, way): nz // 2 - (j ^ way) for j in range(2) for way in range(2)}
    y_hops = {(j, way): ny // 2 - (j ^ way) for j in range(2) for way in range(2)}

    def chain(own_part, at, size, at_me, hops, buffers, sems, j, way, k):
        sign = 1 if way == 0 else size - 1
        out, arrived = buffers
        if k:
            copy(out.at[j, way, k - 1], arrived.at[j, way, k - 1], sems[0].at[j, way, k - 1], sems[1].at[j, way, k - 1], at(sign)[1]).wait_recv()
        if k == hops[j, way]:
            return arrived[j, way, k - 1].astype(F32)
        total = own_part(j, (at_me + sign * (hops[j, way] - k)) % size)
        if k:
            total = total + arrived[j, way, k - 1].astype(F32)
        out[j, way, k] = total.astype(BF16)
        send(out.at[j, way, k], arrived.at[j, way, k], sems[0].at[j, way, k], sems[1].at[j, way, k], at(sign)[1])

    step_z = functools.partial(chain, own_z, at_z, nz, z, z_hops, (zc, zr), (zc_s, zc_r))
    step_w = functools.partial(chain, own_w, at_z, nz, z, z_hops, (wc, wr), (wc_s, wc_r))
    step_y = functools.partial(chain, own_y, at_y, ny, y, y_hops, (yc, yr), (yc_s, yc_r))

    other_half(2)
    pl.semaphore_wait(barrier, len(peers))
    start_swap(2)

    fills[1].wait()
    smz[...] = jnp.zeros_like(smz)
    for i in range(nz):
        smz[i, 0:SMALL_ROWS, :] = small[:, i * 128 : (i + 1) * 128].astype(F32)
    smr[z] = smz[z]
    for d in range(1, nz):
        zz, peer = at_z(d)
        send(smz.at[zz], smr.at[z], smz_s.at[d], smz_r.at[z], peer)

    own_half(2)
    other_half(1)
    start_swap(1)
    swap(2).wait_recv()
    step_y(0, 0, 0)
    step_y(1, 1, 0)
    own_half(1)
    other_half(3)
    start_swap(3)
    swap(1).wait_recv()
    step_y(1, 0, 0)
    own_half(3)
    other_half(0)
    start_swap(0)
    swap(3).wait_recv()
    step_y(0, 1, 0)
    own_half(0)
    swap(0).wait_recv()
    for j, way in z_hops:
        step_z(j, way, 0)
    step_y(0, 0, 1)
    step_y(1, 1, 1)

    for d in range(1, nz):
        zz, peer = at_z(d)
        copy(smz.at[zz], smr.at[zz], smz_s.at[d], smz_r.at[zz], peer).wait_recv()
    block = smr[0]
    for i in range(1, nz):
        block = block + smr[i]
    smc[c] = block
    send(smc.at[c], smc.at[c], smc_s.at[0], smc_r.at[c], sibling)

    def steps(step, k):
        for j, way in z_hops:
            if k < z_hops[j, way]:
                step(j, way, k)

    steps(step_z, 1)
    copy(smc.at[c], smc.at[other], smc_s.at[0], smc_r.at[other], sibling).wait_recv()
    smy[y] = smc[0] + smc[1]
    for d in range(1, ny):
        yy, peer = at_y(d)
        send(smy.at[y], smy.at[y], smy_s.at[d], smy_r.at[y], peer)

    for j in range(2):
        total = own_y(j, y)
        for way in range(2):
            total = total + step_y(j, way, y_hops[j, way])
        szf[:, :, columns(j)] = total
    steps(step_w, 0)
    steps(step_z, 2)
    steps(step_w, 1)
    for k in range(3, nz // 2):
        steps(step_z, k)
    for d in range(1, ny):
        yy, peer = at_y(d)
        copy(smy.at[y], smy.at[yy], smy_s.at[d], smy_r.at[yy], peer).wait_recv()
    block = smy[0]
    for i in range(1, ny):
        block = block + smy[i]
    smf[z] = block
    for d in range(1, nz):
        zz, peer = at_z(d)
        send(smf.at[z], smf.at[z], smf_s.at[d], smf_r.at[z], peer)
    steps(step_w, 2)

    for j in range(2):
        total = own_z(j, z)
        for way in range(2):
            total = total + step_z(j, way, z_hops[j, way])
        syf[:, :, columns(j)] = total
        sy[:, :, columns(j)] = total.astype(BF16)
    for d in range(1, ny):
        yy, peer = at_y(d)
        send(sy.at[yy], ry.at[y], sy_s.at[d], sy_r.at[y], peer)
    for k in range(3, nz // 2):
        steps(step_w, k)

    def place(total, start, j):
        for q in range(2):
            own_grad[pl.ds(4 * start + 2 * q + j, total.shape[0], stride=4), :] = total[:, q * 128 : (q + 1) * 128]

    for d in range(1, nz):
        zz, peer = at_z(d)
        copy(smf.at[z], smf.at[zz], smf_s.at[d], smf_r.at[zz], peer).wait_recv()
    small_square = jnp.zeros((8, 128), F32)
    for i in range(nz):
        rows = smf[i]
        small_square = small_square + folded(rows * rows)
    for d in range(1, ny):
        yy, peer = at_y(d)
        copy(sy.at[yy], ry.at[yy], sy_s.at[d], sy_r.at[yy], peer).wait_recv()
    for j in range(2):
        total = syf[y, :, columns(j)]
        for d in range(1, ny):
            total = total + ry[(y + d) % ny, :, columns(j)].astype(F32)
        place(total, 0, j)
    for j in range(2):
        total = own_w(j, z)
        for way in range(2):
            total = total + step_w(j, way, z_hops[j, way])
        place(total, Z_FIRST, j)

    for fill in fills[2:]:
        fill.wait()
    grad = own_grad[...]
    here = z * 2 + c
    nzc[here] = folded(grad * grad)
    for d in range(1, 2 * nz):
        there, peer = at_zc(d)
        send(nzc.at[here], nzc.at[here], nzc_s.at[d], nzc_r.at[here], peer)
    for d in range(1, 2 * nz):
        there, peer = at_zc(d)
        copy(nzc.at[here], nzc.at[there], nzc_s.at[d], nzc_r.at[there], peer).wait_recv()
    part = small_square * (1.0 / ny)
    for i in range(2 * nz):
        part = part + nzc[i]
    here = y * nx + x
    nyx[here] = part
    for d in range(1, ny * nx):
        there, peer = at_yx(d)
        send(nyx.at[here], nyx.at[here], nyx_s.at[d], nyx_r.at[here], peer)
    for d in range(1, ny * nx):
        there, peer = at_yx(d)
        copy(nyx.at[here], nyx.at[there], nyx_s.at[d], nyx_r.at[there], peer).wait_recv()
    part = nyx[0]
    for i in range(1, ny * nx):
        part = part + nyx[i]
    total = jnp.sum(part, keepdims=True)
    limit = clip_factor * math.sqrt(2 * D * KV_COLS + SMALL_ROWS * D)
    scale = jnp.minimum(1.0, limit / (jnp.sqrt(total) + 1e-06))

    master_new, first_new, second_new = adamw(grad, scale, m1[...], m2[...], mw[...], weight_decay)
    gat[y, c, z] = master_new.astype(BF16)

    def z_block(core, zz, half):
        return gat.at[:, core, zz, half * (LAST_Z // 2) : (half + 1) * (LAST_Z // 2)]

    def piece(core, yy, zz):
        return gat.at[yy, core, zz, LAST_Z:256]

    def half_piece(core, yy, zz, way):
        middle = (LAST_Z + 256) // 2
        return gat.at[yy, core, zz, slice(LAST_Z, middle) if way == 0 else slice(middle, 256)]

    def on_both_y(zz):
        for way in range(2):
            part = piece(c, y, zz)
            send(part, part, b2_s.at[way, zz], b2_r.at[way, zz], at_y(1 if way == 0 else ny - 1)[1])
        send(piece(c, y, zz), piece(c, y, zz), fb_s.at[0, zz], fb_r.at[0, zz], sibling)

    def relay_y(zz):
        for way in range(2):
            sign = 1 if way == 0 else ny - 1
            behind, source = at_y(ny - sign)
            part = piece(c, behind, zz)
            copy(part, part, b2_s.at[way, zz], b2_r.at[way, zz], source).wait_recv()
            half = half_piece(c, behind, zz, way)
            send(half, half, b3_s.at[way, zz], b3_r.at[way, zz], at_y(sign)[1])
            send(part, part, fb_s.at[1 + way, zz], fb_r.at[1 + way, zz], sibling)

    def far_y(zz):
        across, source = at_y(ny // 2)
        for way in range(2):
            half = half_piece(c, across, zz, way)
            copy(half, half, b3_s.at[way, zz], b3_r.at[way, zz], source).wait_recv()
        send(piece(c, across, zz), piece(c, across, zz), fb_s.at[3, zz], fb_r.at[3, zz], sibling)

    b_hops = (nz // 2, nz // 2 - 1)

    def step_b(way, k):
        sign = 1 if way == 0 else nz - 1
        zz = (z + (nz - sign) * k) % nz
        part = piece(c, y, zz)
        if k:
            copy(part, part, b1_s.at[way, k - 1], b1_r.at[way, k - 1], at_z(nz - sign)[1]).wait_recv()
        if k < b_hops[way]:
            send(part, part, b1_s.at[way, k], b1_r.at[way, k], at_z(sign)[1])
        if k or way == 0:
            on_both_y(zz)

    def step_g(half, way, k):
        sign = 1 if way == 0 else nz - 1
        zz = (z + (nz - sign) * k) % nz
        part = z_block(c, zz, half)
        if k:
            copy(part, part, gc_s.at[half, way, k - 1], gc_r.at[half, way, k - 1], at_z(nz - sign)[1]).wait_recv()
        if k < z_hops[half, way]:
            send(part, part, gc_s.at[half, way, k], gc_r.at[half, way, k], at_z(sign)[1])
        if k or way == 0:
            send(part, part, fa_s.at[half, way, k], fa_r.at[half, way, k], sibling)

    def around(k):
        return [(z + (nz - k if way == 0 else k)) % nz for way in range(2) if k <= b_hops[way] and (k or way == 0)]

    step_b(0, 0)
    step_b(1, 0)
    for d in range(1, ny):
        yy, peer = at_y(d)
        part = gat.at[y, c, z, 0:LAST_Z]
        send(part, part, a1_s.at[d], a1_r.at[y], peer)

    om[...] = master_new
    o1[...] = first_new
    o2[...] = second_new

    for d in range(1, ny):
        yy, peer = at_y(d)
        part = gat.at[yy, c, z, 0:LAST_Z]
        copy(part, part, a1_s.at[d], a1_r.at[yy], peer).wait_recv()
    for half, way in z_hops:
        step_g(half, way, 0)
    decay = jnp.where(lax.broadcasted_iota(jnp.int32, (SMALL_ROWS, 128), 0) < EXPERTS, weight_decay, 0.0).astype(F32)
    for k in range(1, nz // 2 + 1):
        for way in range(2):
            if k <= b_hops[way]:
                step_b(way, k)
        for half, way in z_hops:
            if k <= z_hops[half, way]:
                step_g(half, way, k)
        for zz in around(k - 1):
            relay_y(zz)
        for zz in around(k - 2) if k > 1 else ():
            far_y(zz)
        if k == 1:
            for i in range(nz):
                lanes = slice(i * 128, (i + 1) * 128)
                made = adamw(smf[i, 0:SMALL_ROWS, :], scale, s1[:, lanes], s2[:, lanes], sm[:, lanes], decay)
                osm[:, lanes], os1[:, lanes], os2[:, lanes] = made
                osw[:, lanes] = made[0].astype(BF16)
    for zz in around(nz // 2):
        relay_y(zz)
    for k in (nz // 2 - 1, nz // 2):
        for zz in around(k):
            far_y(zz)

    for half, way in z_hops:
        for k in range(way, z_hops[half, way] + 1):
            zz = (z + (nz - k if way == 0 else k)) % nz
            copy(z_block(c, zz, half), z_block(other, zz, half), fa_s.at[half, way, k], fa_r.at[half, way, k], sibling).wait_recv()
    for i, d in enumerate((0, ny - 1, 1, ny // 2)):
        yy, _ = at_y(d)
        for zz in range(nz):
            copy(piece(c, yy, zz), piece(other, yy, zz), fb_s.at[i, zz], fb_r.at[i, zz], sibling).wait_recv()
    for made in sent:
        made.wait_send()


def leave(count, *refs):
    semaphores = refs[2 * count]
    copies = [pltpu.make_async_copy(refs[i], refs[count + i], semaphores.at[i]) for i in range(count)]
    for made in copies:
        made.start()
    for made in copies:
        made.wait()


def stored(array):
    rows = array.shape[0]
    return array.reshape(rows, 2, 2, 128).transpose(0, 2, 1, 3).reshape(rows * 4, 128)


def unstored(array):
    rows = array.shape[0] // 4
    return array.reshape(rows, 2, 2, 128).transpose(0, 2, 1, 3).reshape(rows, 2, 256)


def body(
    ny, nx, nz,
    normed_inputs,
    projection_cotangent,
    small_partials,
    master_weights,
    first_moment,
    second_moment,
    small_master,
    small_first,
    small_second,
):
    tokens, features = normed_inputs.shape
    assert ny == 4 and features == ny * 2 * nz * ROWS
    small_shape = jax.ShapeDtypeStruct(small_master.shape, F32)
    owned = jax.ShapeDtypeStruct((4 * ROWS, 128), F32)
    dma = pltpu.SemaphoreType.DMA
    vm = pltpu.VMEM
    last = ROWS - Z_FIRST
    along_y, along_z = [dma((ny,))] * 2, [dma((nz,))] * 2
    pairs, chains = [dma((2,))] * 2, [dma((2, 2, nz // 2))] * 2
    given = (
        normed_inputs, stored(projection_cotangent), small_partials[0],
        stored(master_weights), stored(first_moment), stored(second_moment),
        small_master, small_first, small_second,
    )
    given = [pltpu.with_memory_space_constraint(array, pltpu.HBM) for array in given]
    outs = pl.pallas_call(
        functools.partial(kernel, ny, nx, nz),
        out_shape=(
            owned, owned, owned,
            jax.ShapeDtypeStruct((ny, 2, nz, 4 * ROWS, 128), BF16),
            small_shape, small_shape, small_shape,
            jax.ShapeDtypeStruct(small_master.shape, BF16),
        ),
        in_specs=[pl.BlockSpec(memory_space=pltpu.HBM)] * 9,
        out_specs=[pl.BlockSpec(memory_space=pltpu.VMEM)] * 8,
        scratch_shapes=[
            *[vm(array.shape, array.dtype) for array in given[1:]],
            vm((2 * ny, tokens, nz * ROWS), BF16),
            vm((4 * tokens, 128), F32),
            vm((tokens, 2 * HALF), BF16),
            vm((ny, nz, ROWS, 2 * HALF), BF16),
            vm((ny, nz, ROWS, 2 * HALF), F32),
            vm((ny, nz, ROWS, 2 * HALF), BF16),
            *[vm((2, 2, nz // 2, ny, Z_FIRST, HALF), BF16)] * 2,
            *[vm((2, 2, ny // 2, nz, last, HALF), BF16)] * 2,
            vm((ny, Z_FIRST, 2 * HALF), BF16),
            vm((ny, Z_FIRST, 2 * HALF), F32),
            vm((ny, Z_FIRST, 2 * HALF), BF16),
            *[vm((2, 2, nz // 2, last, HALF), BF16)] * 2,
            vm((nz, last, 2 * HALF), F32),
            vm((4 * ROWS, 128), F32),
            vm((nz, 16, 128), F32),
            vm((nz, 16, 128), F32),
            vm((2, 16, 128), F32),
            vm((ny, 16, 128), F32),
            vm((nz, 16, 128), F32),
            vm((2 * nz, 8, 128), F32),
            vm((ny * nx, 8, 128), F32),
            dma((8,)), dma((2 * ny,)), *along_y, *chains, *[dma((2, 2, ny // 2))] * 2, *along_y, *chains,
            *along_z, *pairs, *along_y, *along_z,
            *[dma((2 * nz,))] * 2, *[dma((ny * nx,))] * 2,
            *along_y, *[dma((2, nz // 2))] * 2, *chains, *[dma((2, nz))] * 4, *[dma((2, 2, nz // 2 + 1))] * 2, *[dma((4, nz))] * 2,
        ],
        compiler_params=pltpu.CompilerParams(
            collective_id=0, has_side_effects=True, vmem_limit_bytes=36 << 20
        ),
    )(*given)
    count = len(outs)
    outs = pl.pallas_call(
        functools.partial(leave, count),
        out_shape=[jax.ShapeDtypeStruct(o.shape, o.dtype) for o in outs],
        in_specs=[pl.BlockSpec(memory_space=pltpu.VMEM)] * count,
        out_specs=[pl.BlockSpec(memory_space=pl.ANY)] * count,
        scratch_shapes=[dma((count,))],
        compiler_params=pltpu.CompilerParams(vmem_limit_bytes=16 << 20),
    )(*outs)
    return (
        unstored(outs[0]), unstored(outs[1]), unstored(outs[2]),
        unstored(outs[3].reshape(-1, 128)),
        outs[4], outs[5], outs[6], outs[7],
    )


def solution(mesh):
    ny, nx, nz = mesh.shape["shard"] // 2, mesh.shape["tensor"], mesh.shape["section"]
    rows = P(("shard", "section"), None, "tensor")
    flat = P(None, "tensor")
    return jax.shard_map(
        functools.partial(body, ny, nx, nz),
        mesh=mesh,
        in_specs=(P(("shard", "section"), None), rows, rows, rows, rows, rows, flat, flat, flat),
        out_specs=(rows, rows, rows, P(None, None, "tensor"), flat, flat, flat, flat),
        check_vma=False,
    )
```

```python
import functools
import math

import jax
import jax.numpy as jnp
from jax import lax
from jax.experimental import pallas as pl
from jax.experimental.pallas import tpu as pltpu
from jax.sharding import PartitionSpec as P

D = 4096
EXPERTS = 8
STEP = 10
KV_COLS = 1024
SMALL_ROWS = 10

beta_one = 0.9
beta_two = 0.95
learning_rate = 0.01
weight_decay = 0.1
epsilon = 1e-08
clip_factor = 0.5

F32 = jnp.float32
BF16 = jnp.bfloat16
MESH = pl.DeviceIdType.MESH

ROWS = 64
HALF = 256
Z_FIRST = 32
LAST_Z = 32


def adamw(gradient, scale, first, second, master, decay):
    clipped = gradient * scale
    first_new = beta_one * first + (1.0 - beta_one) * clipped
    second_new = beta_two * second + (1.0 - beta_two) * clipped * clipped
    first_hat = first_new / (1.0 - beta_one**STEP)
    second_hat = second_new / (1.0 - beta_two**STEP)
    master_new = master - learning_rate * (
        first_hat / (jnp.sqrt(second_hat) + epsilon) + decay * master
    )
    return (master_new, first_new, second_new)


def folded(square):
    return square.reshape(-1, 8, 128).sum(axis=0)


def kernel(
    ny, nx, nz,
    inputs, *refs,
):
    held = refs[:8]
    om, o1, o2, gat, osm, os1, os2, osw = refs[8:16]
    cotangent, small, mw, m1, m2, sm, s1, s2 = refs[16:24]
    (
        xv, wide, flat, gs, own, pair, zc, zr, yc, yr, sy, syf, ry, wc, wr, szf, own_grad,
        smz, smr, smc, smy, smf, nzc, nyx,
        in_s, x_s, pair_s, pair_r, zc_s, zc_r, yc_s, yc_r, sy_s, sy_r, wc_s, wc_r,
        smz_s, smz_r, smc_s, smc_r, smy_s, smy_r, smf_s, smf_r,
        nzc_s, nzc_r, nyx_s, nyx_r,
        a1_s, a1_r, b1_s, b1_r, gc_s, gc_r, b2_s, b2_r, b3_s, b3_r, fa_s, fa_r, fb_s, fb_r,
    ) = refs[24:]
    shard = lax.axis_index("shard")
    x = lax.axis_index("tensor")
    z = lax.axis_index("section")
    y, c = shard // 2, shard % 2
    other = 1 - c
    sibling = (y * 2 + other, x, z)

    def at_y(d):
        yy = (y + d) % ny
        return yy, (yy * 2 + c, x, z)

    def at_z(d):
        zz = (z + d) % nz
        return zz, (shard, x, zz)

    def at_zc(d):
        zz, cc = (z + d // 2) % nz, (c + d % 2) % 2
        return zz * 2 + cc, (y * 2 + cc, x, zz)

    def at_yx(d):
        yy, xx = (y + d // nx) % ny, (x + d % nx) % nx
        return yy * nx + xx, (yy * 2 + c, xx, z)

    def copy(src, dst, send, recv, device):
        return pltpu.make_async_remote_copy(
            src_ref=src, dst_ref=dst, send_sem=send, recv_sem=recv, device_id=device, device_id_type=MESH
        )

    sent = []

    def send(*a):
        made = copy(*a)
        made.start()
        sent.append(made)

    fills = [pltpu.make_async_copy(held[i], refs[16 + i], in_s.at[i]) for i in range(8)]
    fills[0].start()

    order = (2, 1, 3, 0)
    loads = {}
    for i, d in enumerate(order):
        for half, core in enumerate((other, c)):
            start = pl.multiple_of((at_y(d)[0] * 2 + core) * (nz * ROWS), nz * ROWS)
            slot = 2 * i + half
            loads[d, half] = slot, pltpu.make_async_copy(
                inputs.at[:, pl.ds(start, nz * ROWS)], xv.at[slot], x_s.at[slot]
            )
            if slot < 3:
                loads[d, half][1].start()

    for fill in fills[1:]:
        fill.start()

    barrier = pltpu.get_barrier_semaphore()
    peers = [at_zc(d)[1] for d in range(1, 2 * nz)] + [at_yx(d)[1] for d in range(1, ny * nx)]
    for peer in peers:
        pl.semaphore_signal(barrier, inc=1, device_id=peer, device_id_type=MESH)

    tokens = flat.shape[0]
    fills[0].wait()
    wide[...] = cotangent[...].astype(F32)
    for j in range(2):
        for q in range(2):
            flat[:, j * HALF + q * 128 : j * HALF + (q + 1) * 128] = wide[
                pl.ds(2 * q + j, tokens, stride=4), :
            ].astype(BF16)

    def summed(d, half):
        slot, load = loads[d, half]
        load.wait()
        for later, following in loads.values():
            if later == slot + 3:
                following.start()
        made = lax.dot_general(
            xv[slot], flat[...], (((0,), (0,)), ((), ())), preferred_element_type=F32
        )
        return made.reshape(nz, ROWS, 2 * HALF)

    def swap(d):
        yy, _ = at_y(d)
        return copy(gs.at[yy], pair.at[yy], pair_s.at[d], pair_r.at[yy], sibling)

    def other_half(d):
        gs[at_y(d)[0]] = summed(d, 0).astype(BF16)

    def own_half(d):
        own[at_y(d)[0]] = summed(d, 1)

    def start_swap(d):
        made = swap(d)
        made.start()
        sent.append(made)

    def columns(j):
        return slice(j * HALF, (j + 1) * HALF)

    def own_z(j, zz):
        rows = slice(0, Z_FIRST)
        return own[:, zz, rows, columns(j)] + pair[:, zz, rows, columns(j)].astype(F32)

    def own_y(j, yy):
        rows = slice(Z_FIRST, ROWS)
        return own[yy, :, rows, columns(j)] + pair[yy, :, rows, columns(j)].astype(F32)

    def own_w(j, zz):
        return szf[zz, :, columns(j)]

    z_hops = {(j, way): nz // 2 - (j ^ way) for j in range(2) for way in range(2)}
    y_hops = {(j, way): ny // 2 - (j ^ way) for j in range(2) for way in range(2)}

    def chain(own_part, at, size, at_me, hops, buffers, sems, j, way, k):
        sign = 1 if way == 0 else size - 1
        out, arrived = buffers
        if k:
            copy(out.at[j, way, k - 1], arrived.at[j, way, k - 1], sems[0].at[j, way, k - 1], sems[1].at[j, way, k - 1], at(sign)[1]).wait_recv()
        if k == hops[j, way]:
            return arrived[j, way, k - 1].astype(F32)
        total = own_part(j, (at_me + sign * (hops[j, way] - k)) % size)
        if k:
            total = total + arrived[j, way, k - 1].astype(F32)
        out[j, way, k] = total.astype(BF16)
        send(out.at[j, way, k], arrived.at[j, way, k], sems[0].at[j, way, k], sems[1].at[j, way, k], at(sign)[1])

    step_z = functools.partial(chain, own_z, at_z, nz, z, z_hops, (zc, zr), (zc_s, zc_r))
    step_w = functools.partial(chain, own_w, at_z, nz, z, z_hops, (wc, wr), (wc_s, wc_r))
    step_y = functools.partial(chain, own_y, at_y, ny, y, y_hops, (yc, yr), (yc_s, yc_r))

    other_half(2)
    pl.semaphore_wait(barrier, len(peers))
    start_swap(2)

    fills[1].wait()
    smz[...] = jnp.zeros_like(smz)
    for i in range(nz):
        smz[i, 0:SMALL_ROWS, :] = small[:, i * 128 : (i + 1) * 128].astype(F32)
    smr[z] = smz[z]
    for d in range(1, nz):
        zz, peer = at_z(d)
        send(smz.at[zz], smr.at[z], smz_s.at[d], smz_r.at[z], peer)

    own_half(2)
    other_half(1)
    start_swap(1)
    swap(2).wait_recv()
    step_y(0, 0, 0)
    step_y(1, 1, 0)
    own_half(1)
    other_half(3)
    start_swap(3)
    swap(1).wait_recv()
    step_y(1, 0, 0)
    own_half(3)
    other_half(0)
    start_swap(0)
    swap(3).wait_recv()
    step_y(0, 1, 0)
    own_half(0)
    swap(0).wait_recv()
    for j, way in z_hops:
        step_z(j, way, 0)
    step_y(0, 0, 1)
    step_y(1, 1, 1)

    for d in range(1, nz):
        zz, peer = at_z(d)
        copy(smz.at[zz], smr.at[zz], smz_s.at[d], smz_r.at[zz], peer).wait_recv()
    block = smr[0]
    for i in range(1, nz):
        block = block + smr[i]
    smc[c] = block
    send(smc.at[c], smc.at[c], smc_s.at[0], smc_r.at[c], sibling)

    def steps(step, k):
        for j, way in z_hops:
            if k < z_hops[j, way]:
                step(j, way, k)

    steps(step_z, 1)
    copy(smc.at[c], smc.at[other], smc_s.at[0], smc_r.at[other], sibling).wait_recv()
    smy[y] = smc[0] + smc[1]
    for d in range(1, ny):
        yy, peer = at_y(d)
        send(smy.at[y], smy.at[y], smy_s.at[d], smy_r.at[y], peer)

    for j in range(2):
        total = own_y(j, y)
        for way in range(2):
            total = total + step_y(j, way, y_hops[j, way])
        szf[:, :, columns(j)] = total
    steps(step_w, 0)
    steps(step_z, 2)
    steps(step_w, 1)
    for k in range(3, nz // 2):
        steps(step_z, k)
    for d in range(1, ny):
        yy, peer = at_y(d)
        copy(smy.at[y], smy.at[yy], smy_s.at[d], smy_r.at[yy], peer).wait_recv()
    block = smy[0]
    for i in range(1, ny):
        block = block + smy[i]
    smf[z] = block
    for d in range(1, nz):
        zz, peer = at_z(d)
        send(smf.at[z], smf.at[z], smf_s.at[d], smf_r.at[z], peer)
    steps(step_w, 2)

    for j in range(2):
        total = own_z(j, z)
        for way in range(2):
            total = total + step_z(j, way, z_hops[j, way])
        syf[:, :, columns(j)] = total
        sy[:, :, columns(j)] = total.astype(BF16)
    for d in range(1, ny):
        yy, peer = at_y(d)
        send(sy.at[yy], ry.at[y], sy_s.at[d], sy_r.at[y], peer)
    for k in range(3, nz // 2):
        steps(step_w, k)

    def place(total, start, j):
        for q in range(2):
            own_grad[pl.ds(4 * start + 2 * q + j, total.shape[0], stride=4), :] = total[:, q * 128 : (q + 1) * 128]

    for d in range(1, nz):
        zz, peer = at_z(d)
        copy(smf.at[z], smf.at[zz], smf_s.at[d], smf_r.at[zz], peer).wait_recv()
    small_square = jnp.zeros((8, 128), F32)
    for i in range(nz):
        rows = smf[i]
        small_square = small_square + folded(rows * rows)
    for d in range(1, ny):
        yy, peer = at_y(d)
        copy(sy.at[yy], ry.at[yy], sy_s.at[d], sy_r.at[yy], peer).wait_recv()
    for j in range(2):
        total = syf[y, :, columns(j)]
        for d in range(1, ny):
            total = total + ry[(y + d) % ny, :, columns(j)].astype(F32)
        place(total, 0, j)
    for j in range(2):
        total = own_w(j, z)
        for way in range(2):
            total = total + step_w(j, way, z_hops[j, way])
        place(total, Z_FIRST, j)

    for fill in fills[2:]:
        fill.wait()
    grad = own_grad[...]
    here = z * 2 + c
    nzc[here] = folded(grad * grad)
    for d in sorted(range(1, 2 * nz), key=lambda d: -min(d // 2, nz - d // 2)):
        there, peer = at_zc(d)
        send(nzc.at[here], nzc.at[here], nzc_s.at[d], nzc_r.at[here], peer)
    for d in range(1, 2 * nz):
        there, peer = at_zc(d)
        copy(nzc.at[here], nzc.at[there], nzc_s.at[d], nzc_r.at[there], peer).wait_recv()
    part = small_square * (1.0 / ny)
    for i in range(2 * nz):
        part = part + nzc[i]
    here = y * nx + x
    nyx[here] = part
    for d in sorted(range(1, ny * nx), key=lambda d: -min(d // nx, ny - d // nx) - min(d % nx, nx - d % nx)):
        there, peer = at_yx(d)
        send(nyx.at[here], nyx.at[here], nyx_s.at[d], nyx_r.at[here], peer)
    for d in range(1, ny * nx):
        there, peer = at_yx(d)
        copy(nyx.at[here], nyx.at[there], nyx_s.at[d], nyx_r.at[there], peer).wait_recv()
    part = nyx[0]
    for i in range(1, ny * nx):
        part = part + nyx[i]
    total = jnp.sum(part, keepdims=True)
    limit = clip_factor * math.sqrt(2 * D * KV_COLS + SMALL_ROWS * D)
    scale = jnp.minimum(1.0, limit / (jnp.sqrt(total) + 1e-06))

    master_new, first_new, second_new = adamw(grad, scale, m1[...], m2[...], mw[...], weight_decay)
    gat[y, c, z] = master_new.astype(BF16)

    def z_block(core, zz, half):
        return gat.at[:, core, zz, half * (LAST_Z // 2) : (half + 1) * (LAST_Z // 2)]

    def piece(core, yy, zz):
        return gat.at[yy, core, zz, LAST_Z:256]

    def half_piece(core, yy, zz, way):
        middle = (LAST_Z + 256) // 2
        return gat.at[yy, core, zz, slice(LAST_Z, middle) if way == 0 else slice(middle, 256)]

    def on_both_y(zz):
        for way in range(2):
            part = piece(c, y, zz)
            send(part, part, b2_s.at[way, zz], b2_r.at[way, zz], at_y(1 if way == 0 else ny - 1)[1])
        send(piece(c, y, zz), piece(c, y, zz), fb_s.at[0, zz], fb_r.at[0, zz], sibling)

    def relay_y(zz):
        for way in range(2):
            sign = 1 if way == 0 else ny - 1
            behind, source = at_y(ny - sign)
            part = piece(c, behind, zz)
            copy(part, part, b2_s.at[way, zz], b2_r.at[way, zz], source).wait_recv()
            half = half_piece(c, behind, zz, way)
            send(half, half, b3_s.at[way, zz], b3_r.at[way, zz], at_y(sign)[1])
            send(part, part, fb_s.at[1 + way, zz], fb_r.at[1 + way, zz], sibling)

    def far_y(zz):
        across, source = at_y(ny // 2)
        for way in range(2):
            half = half_piece(c, across, zz, way)
            copy(half, half, b3_s.at[way, zz], b3_r.at[way, zz], source).wait_recv()
        send(piece(c, across, zz), piece(c, across, zz), fb_s.at[3, zz], fb_r.at[3, zz], sibling)

    b_hops = (nz // 2, nz // 2 - 1)

    def step_b(way, k):
        sign = 1 if way == 0 else nz - 1
        zz = (z + (nz - sign) * k) % nz
        part = piece(c, y, zz)
        if k:
            copy(part, part, b1_s.at[way, k - 1], b1_r.at[way, k - 1], at_z(nz - sign)[1]).wait_recv()
        if k < b_hops[way]:
            send(part, part, b1_s.at[way, k], b1_r.at[way, k], at_z(sign)[1])
        if k or way == 0:
            on_both_y(zz)

    def step_g(half, way, k):
        sign = 1 if way == 0 else nz - 1
        zz = (z + (nz - sign) * k) % nz
        part = z_block(c, zz, half)
        if k:
            copy(part, part, gc_s.at[half, way, k - 1], gc_r.at[half, way, k - 1], at_z(nz - sign)[1]).wait_recv()
        if k < z_hops[half, way]:
            send(part, part, gc_s.at[half, way, k], gc_r.at[half, way, k], at_z(sign)[1])
        if k or way == 0:
            send(part, part, fa_s.at[half, way, k], fa_r.at[half, way, k], sibling)

    def around(k):
        return [(z + (nz - k if way == 0 else k)) % nz for way in range(2) if k <= b_hops[way] and (k or way == 0)]

    step_b(0, 0)
    step_b(1, 0)
    for d in range(1, ny):
        yy, peer = at_y(d)
        part = gat.at[y, c, z, 0:LAST_Z]
        send(part, part, a1_s.at[d], a1_r.at[y], peer)

    om[...] = master_new
    o1[...] = first_new
    o2[...] = second_new

    for d in range(1, ny):
        yy, peer = at_y(d)
        part = gat.at[yy, c, z, 0:LAST_Z]
        copy(part, part, a1_s.at[d], a1_r.at[yy], peer).wait_recv()
    for half, way in z_hops:
        step_g(half, way, 0)
    decay = jnp.where(lax.broadcasted_iota(jnp.int32, (SMALL_ROWS, 128), 0) < EXPERTS, weight_decay, 0.0).astype(F32)
    for k in range(1, nz // 2 + 1):
        for way in range(2):
            if k <= b_hops[way]:
                step_b(way, k)
        for zz in around(k - 1):
            relay_y(zz)
        for half, way in z_hops:
            if k <= z_hops[half, way]:
                step_g(half, way, k)
        for zz in around(k - 2) if k > 1 else ():
            far_y(zz)
        if k == 1:
            for i in range(nz):
                lanes = slice(i * 128, (i + 1) * 128)
                made = adamw(smf[i, 0:SMALL_ROWS, :], scale, s1[:, lanes], s2[:, lanes], sm[:, lanes], decay)
                osm[:, lanes], os1[:, lanes], os2[:, lanes] = made
                osw[:, lanes] = made[0].astype(BF16)
    for zz in around(nz // 2):
        relay_y(zz)
    for k in (nz // 2 - 1, nz // 2):
        for zz in around(k):
            far_y(zz)

    for half, way in z_hops:
        for k in range(way, z_hops[half, way] + 1):
            zz = (z + (nz - k if way == 0 else k)) % nz
            copy(z_block(c, zz, half), z_block(other, zz, half), fa_s.at[half, way, k], fa_r.at[half, way, k], sibling).wait_recv()
    for i, d in enumerate((0, ny - 1, 1, ny // 2)):
        yy, _ = at_y(d)
        for zz in range(nz):
            copy(piece(c, yy, zz), piece(other, yy, zz), fb_s.at[i, zz], fb_r.at[i, zz], sibling).wait_recv()
    for made in sent:
        made.wait_send()


def leave(count, *refs):
    semaphores = refs[2 * count]
    copies = [pltpu.make_async_copy(refs[i], refs[count + i], semaphores.at[i]) for i in range(count)]
    for made in copies:
        made.start()
    for made in copies:
        made.wait()


def stored(array):
    rows = array.shape[0]
    return array.reshape(rows, 2, 2, 128).transpose(0, 2, 1, 3).reshape(rows * 4, 128)


def unstored(array):
    rows = array.shape[0] // 4
    return array.reshape(rows, 2, 2, 128).transpose(0, 2, 1, 3).reshape(rows, 2, 256)


def body(
    ny, nx, nz,
    normed_inputs,
    projection_cotangent,
    small_partials,
    master_weights,
    first_moment,
    second_moment,
    small_master,
    small_first,
    small_second,
):
    tokens, features = normed_inputs.shape
    assert ny == 4 and features == ny * 2 * nz * ROWS
    small_shape = jax.ShapeDtypeStruct(small_master.shape, F32)
    owned = jax.ShapeDtypeStruct((4 * ROWS, 128), F32)
    dma = pltpu.SemaphoreType.DMA
    vm = pltpu.VMEM
    last = ROWS - Z_FIRST
    along_y, along_z = [dma((ny,))] * 2, [dma((nz,))] * 2
    pairs, chains = [dma((2,))] * 2, [dma((2, 2, nz // 2))] * 2
    given = (
        normed_inputs, stored(projection_cotangent), small_partials[0],
        stored(master_weights), stored(first_moment), stored(second_moment),
        small_master, small_first, small_second,
    )
    given = [pltpu.with_memory_space_constraint(array, pltpu.HBM) for array in given]
    outs = pl.pallas_call(
        functools.partial(kernel, ny, nx, nz),
        out_shape=(
            owned, owned, owned,
            jax.ShapeDtypeStruct((ny, 2, nz, 4 * ROWS, 128), BF16),
            small_shape, small_shape, small_shape,
            jax.ShapeDtypeStruct(small_master.shape, BF16),
        ),
        in_specs=[pl.BlockSpec(memory_space=pltpu.HBM)] * 9,
        out_specs=[pl.BlockSpec(memory_space=pltpu.VMEM)] * 8,
        scratch_shapes=[
            *[vm(array.shape, array.dtype) for array in given[1:]],
            vm((2 * ny, tokens, nz * ROWS), BF16),
            vm((4 * tokens, 128), F32),
            vm((tokens, 2 * HALF), BF16),
            vm((ny, nz, ROWS, 2 * HALF), BF16),
            vm((ny, nz, ROWS, 2 * HALF), F32),
            vm((ny, nz, ROWS, 2 * HALF), BF16),
            *[vm((2, 2, nz // 2, ny, Z_FIRST, HALF), BF16)] * 2,
            *[vm((2, 2, ny // 2, nz, last, HALF), BF16)] * 2,
            vm((ny, Z_FIRST, 2 * HALF), BF16),
            vm((ny, Z_FIRST, 2 * HALF), F32),
            vm((ny, Z_FIRST, 2 * HALF), BF16),
            *[vm((2, 2, nz // 2, last, HALF), BF16)] * 2,
            vm((nz, last, 2 * HALF), F32),
            vm((4 * ROWS, 128), F32),
            vm((nz, 16, 128), F32),
            vm((nz, 16, 128), F32),
            vm((2, 16, 128), F32),
            vm((ny, 16, 128), F32),
            vm((nz, 16, 128), F32),
            vm((2 * nz, 8, 128), F32),
            vm((ny * nx, 8, 128), F32),
            dma((8,)), dma((2 * ny,)), *along_y, *chains, *[dma((2, 2, ny // 2))] * 2, *along_y, *chains,
            *along_z, *pairs, *along_y, *along_z,
            *[dma((2 * nz,))] * 2, *[dma((ny * nx,))] * 2,
            *along_y, *[dma((2, nz // 2))] * 2, *chains, *[dma((2, nz))] * 4, *[dma((2, 2, nz // 2 + 1))] * 2, *[dma((4, nz))] * 2,
        ],
        compiler_params=pltpu.CompilerParams(
            collective_id=0, has_side_effects=True, vmem_limit_bytes=36 << 20
        ),
    )(*given)
    count = len(outs)
    outs = pl.pallas_call(
        functools.partial(leave, count),
        out_shape=[jax.ShapeDtypeStruct(o.shape, o.dtype) for o in outs],
        in_specs=[pl.BlockSpec(memory_space=pltpu.VMEM)] * count,
        out_specs=[pl.BlockSpec(memory_space=pl.ANY)] * count,
        scratch_shapes=[dma((count,))],
        compiler_params=pltpu.CompilerParams(vmem_limit_bytes=16 << 20),
    )(*outs)
    return (
        unstored(outs[0]), unstored(outs[1]), unstored(outs[2]),
        unstored(outs[3].reshape(-1, 128)),
        outs[4], outs[5], outs[6], outs[7],
    )


def solution(mesh):
    ny, nx, nz = mesh.shape["shard"] // 2, mesh.shape["tensor"], mesh.shape["section"]
    rows = P(("shard", "section"), None, "tensor")
    flat = P(None, "tensor")
    return jax.shard_map(
        functools.partial(body, ny, nx, nz),
        mesh=mesh,
        in_specs=(P(("shard", "section"), None), rows, rows, rows, rows, rows, flat, flat, flat),
        out_specs=(rows, rows, rows, P(None, None, "tensor"), flat, flat, flat, flat),
        check_vma=False,
    )
```

```python
import functools
import math

import jax
import jax.numpy as jnp
from jax import lax
from jax.experimental import pallas as pl
from jax.experimental.pallas import tpu as pltpu
from jax.sharding import PartitionSpec as P

D = 4096
EXPERTS = 8
STEP = 10
KV_COLS = 1024
SMALL_ROWS = 10

beta_one = 0.9
beta_two = 0.95
learning_rate = 0.01
weight_decay = 0.1
epsilon = 1e-08
clip_factor = 0.5

F32 = jnp.float32
BF16 = jnp.bfloat16
MESH = pl.DeviceIdType.MESH

ROWS = 64
HALF = 256
Z_FIRST = 32
LAST_Z = 32


def adamw(gradient, scale, first, second, master, decay):
    clipped = gradient * scale
    first_new = beta_one * first + (1.0 - beta_one) * clipped
    second_new = beta_two * second + (1.0 - beta_two) * clipped * clipped
    first_hat = first_new / (1.0 - beta_one**STEP)
    second_hat = second_new / (1.0 - beta_two**STEP)
    master_new = master - learning_rate * (
        first_hat / (jnp.sqrt(second_hat) + epsilon) + decay * master
    )
    return (master_new, first_new, second_new)


def folded(square):
    return square.reshape(-1, 8, 128).sum(axis=0)


def kernel(
    ny, nx, nz,
    inputs, *refs,
):
    held = refs[:8]
    om, o1, o2, gat, osm, os1, os2, osw = refs[8:16]
    cotangent, small, mw, m1, m2, sm, s1, s2 = refs[16:24]
    (
        xv, wide, flat, gs, own, pair, zc, zr, yc, yr, sy, syf, ry, wc, wr, szf, own_grad,
        smz, smr, smc, smy, smf, nzc, nyx,
        in_s, x_s, pair_s, pair_r, zc_s, zc_r, yc_s, yc_r, sy_s, sy_r, wc_s, wc_r,
        smz_s, smz_r, smc_s, smc_r, smy_s, smy_r, smf_s, smf_r,
        nzc_s, nzc_r, nyx_s, nyx_r,
        a1_s, a1_r, b1_s, b1_r, gc_s, gc_r, b2_s, b2_r, b3_s, b3_r, fa_s, fa_r, fb_s, fb_r,
    ) = refs[24:]
    shard = lax.axis_index("shard")
    x = lax.axis_index("tensor")
    z = lax.axis_index("section")
    y, c = shard // 2, shard % 2
    other = 1 - c
    sibling = (y * 2 + other, x, z)

    def at_y(d):
        yy = (y + d) % ny
        return yy, (yy * 2 + c, x, z)

    def at_z(d):
        zz = (z + d) % nz
        return zz, (shard, x, zz)

    def at_zc(d):
        zz, cc = (z + d // 2) % nz, (c + d % 2) % 2
        return zz * 2 + cc, (y * 2 + cc, x, zz)

    def at_yx(d):
        yy, xx = (y + d // nx) % ny, (x + d % nx) % nx
        return yy * nx + xx, (yy * 2 + c, xx, z)

    def copy(src, dst, send, recv, device):
        return pltpu.make_async_remote_copy(
            src_ref=src, dst_ref=dst, send_sem=send, recv_sem=recv, device_id=device, device_id_type=MESH
        )

    sent = []

    def send(*a):
        made = copy(*a)
        made.start()
        sent.append(made)

    fills = [pltpu.make_async_copy(held[i], refs[16 + i], in_s.at[i]) for i in range(8)]
    fills[0].start()

    order = (2, 1, 3, 0)
    loads = {}
    for i, d in enumerate(order):
        for half, core in enumerate((other, c)):
            start = pl.multiple_of((at_y(d)[0] * 2 + core) * (nz * ROWS), nz * ROWS)
            slot = 2 * i + half
            loads[d, half] = slot, pltpu.make_async_copy(
                inputs.at[:, pl.ds(start, nz * ROWS)], xv.at[slot], x_s.at[slot]
            )
            if slot < 3:
                loads[d, half][1].start()

    for fill in fills[1:]:
        fill.start()

    barrier = pltpu.get_barrier_semaphore()
    peers = [at_zc(d)[1] for d in range(1, 2 * nz)] + [at_yx(d)[1] for d in range(1, ny * nx)]
    for peer in peers:
        pl.semaphore_signal(barrier, inc=1, device_id=peer, device_id_type=MESH)

    tokens = flat.shape[0]
    fills[0].wait()
    wide[...] = cotangent[...].astype(F32)
    for j in range(2):
        for q in range(2):
            flat[:, j * HALF + q * 128 : j * HALF + (q + 1) * 128] = wide[
                pl.ds(2 * q + j, tokens, stride=4), :
            ].astype(BF16)

    def summed(d, half):
        slot, load = loads[d, half]
        load.wait()
        for later, following in loads.values():
            if later == slot + 3:
                following.start()
        made = lax.dot_general(
            xv[slot], flat[...], (((0,), (0,)), ((), ())), preferred_element_type=F32
        )
        return made.reshape(nz, ROWS, 2 * HALF)

    def swap(d):
        yy, _ = at_y(d)
        return copy(gs.at[yy], pair.at[yy], pair_s.at[d], pair_r.at[yy], sibling)

    def other_half(d):
        gs[at_y(d)[0]] = summed(d, 0).astype(BF16)

    def own_half(d):
        own[at_y(d)[0]] = summed(d, 1)

    def start_swap(d):
        made = swap(d)
        made.start()
        sent.append(made)

    def columns(j):
        return slice(j * HALF, (j + 1) * HALF)

    def own_z(j, zz):
        rows = slice(0, Z_FIRST)
        return own[:, zz, rows, columns(j)] + pair[:, zz, rows, columns(j)].astype(F32)

    def own_y(j, yy):
        rows = slice(Z_FIRST, ROWS)
        return own[yy, :, rows, columns(j)] + pair[yy, :, rows, columns(j)].astype(F32)

    def own_w(j, zz):
        return szf[zz, :, columns(j)]

    z_hops = {(j, way): nz // 2 - (j ^ way) for j in range(2) for way in range(2)}
    y_hops = {(j, way): ny // 2 - (j ^ way) for j in range(2) for way in range(2)}

    def chain(own_part, at, size, at_me, hops, buffers, sems, j, way, k):
        sign = 1 if way == 0 else size - 1
        out, arrived = buffers
        if k:
            copy(out.at[j, way, k - 1], arrived.at[j, way, k - 1], sems[0].at[j, way, k - 1], sems[1].at[j, way, k - 1], at(sign)[1]).wait_recv()
        if k == hops[j, way]:
            return arrived[j, way, k - 1].astype(F32)
        total = own_part(j, (at_me + sign * (hops[j, way] - k)) % size)
        if k:
            total = total + arrived[j, way, k - 1].astype(F32)
        out[j, way, k] = total.astype(BF16)
        send(out.at[j, way, k], arrived.at[j, way, k], sems[0].at[j, way, k], sems[1].at[j, way, k], at(sign)[1])

    step_z = functools.partial(chain, own_z, at_z, nz, z, z_hops, (zc, zr), (zc_s, zc_r))
    step_w = functools.partial(chain, own_w, at_z, nz, z, z_hops, (wc, wr), (wc_s, wc_r))
    step_y = functools.partial(chain, own_y, at_y, ny, y, y_hops, (yc, yr), (yc_s, yc_r))

    other_half(2)
    pl.semaphore_wait(barrier, len(peers))
    start_swap(2)

    fills[1].wait()
    smz[...] = jnp.zeros_like(smz)
    for i in range(nz):
        smz[i, 0:SMALL_ROWS, :] = small[:, i * 128 : (i + 1) * 128].astype(F32)
    smr[z] = smz[z]
    for d in range(1, nz):
        zz, peer = at_z(d)
        send(smz.at[zz], smr.at[z], smz_s.at[d], smz_r.at[z], peer)

    own_half(2)
    other_half(1)
    start_swap(1)
    swap(2).wait_recv()
    step_y(0, 0, 0)
    step_y(1, 1, 0)
    own_half(1)
    other_half(3)
    start_swap(3)
    swap(1).wait_recv()
    step_y(1, 0, 0)
    own_half(3)
    other_half(0)
    start_swap(0)
    swap(3).wait_recv()
    step_y(0, 1, 0)
    own_half(0)
    swap(0).wait_recv()
    for j, way in z_hops:
        step_z(j, way, 0)
    step_y(0, 0, 1)
    step_y(1, 1, 1)

    for d in range(1, nz):
        zz, peer = at_z(d)
        copy(smz.at[zz], smr.at[zz], smz_s.at[d], smz_r.at[zz], peer).wait_recv()
    block = smr[0]
    for i in range(1, nz):
        block = block + smr[i]
    smc[c] = block
    send(smc.at[c], smc.at[c], smc_s.at[0], smc_r.at[c], sibling)

    def steps(step, k):
        for j, way in z_hops:
            if k < z_hops[j, way]:
                step(j, way, k)

    steps(step_z, 1)
    copy(smc.at[c], smc.at[other], smc_s.at[0], smc_r.at[other], sibling).wait_recv()
    smy[y] = smc[0] + smc[1]
    for d in range(1, ny):
        yy, peer = at_y(d)
        send(smy.at[y], smy.at[y], smy_s.at[d], smy_r.at[y], peer)

    for j in range(2):
        total = own_y(j, y)
        for way in range(2):
            total = total + step_y(j, way, y_hops[j, way])
        szf[:, :, columns(j)] = total
    steps(step_w, 0)
    steps(step_z, 2)
    steps(step_w, 1)
    for k in range(3, nz // 2):
        steps(step_z, k)
    for d in range(1, ny):
        yy, peer = at_y(d)
        copy(smy.at[y], smy.at[yy], smy_s.at[d], smy_r.at[yy], peer).wait_recv()
    block = smy[0]
    for i in range(1, ny):
        block = block + smy[i]
    smf[z] = block
    for d in range(1, nz):
        zz, peer = at_z(d)
        send(smf.at[z], smf.at[z], smf_s.at[d], smf_r.at[z], peer)
    steps(step_w, 2)

    for j in range(2):
        total = own_z(j, z)
        for way in range(2):
            total = total + step_z(j, way, z_hops[j, way])
        syf[:, :, columns(j)] = total
        sy[:, :, columns(j)] = total.astype(BF16)
    for d in range(1, ny):
        yy, peer = at_y(d)
        send(sy.at[yy], ry.at[y], sy_s.at[d], sy_r.at[y], peer)
    for k in range(3, nz // 2):
        steps(step_w, k)

    def place(total, start, j):
        for q in range(2):
            own_grad[pl.ds(4 * start + 2 * q + j, total.shape[0], stride=4), :] = total[:, q * 128 : (q + 1) * 128]

    for d in range(1, nz):
        zz, peer = at_z(d)
        copy(smf.at[z], smf.at[zz], smf_s.at[d], smf_r.at[zz], peer).wait_recv()
    small_square = jnp.zeros((8, 128), F32)
    for i in range(nz):
        rows = smf[i]
        small_square = small_square + folded(rows * rows)
    for d in range(1, ny):
        yy, peer = at_y(d)
        copy(sy.at[yy], ry.at[yy], sy_s.at[d], sy_r.at[yy], peer).wait_recv()
    for j in range(2):
        total = syf[y, :, columns(j)]
        for d in range(1, ny):
            total = total + ry[(y + d) % ny, :, columns(j)].astype(F32)
        place(total, 0, j)
    for j in range(2):
        total = own_w(j, z)
        for way in range(2):
            total = total + step_w(j, way, z_hops[j, way])
        place(total, Z_FIRST, j)

    for fill in fills[2:]:
        fill.wait()
    grad = own_grad[...]
    here = z * 2 + c
    nzc[here] = folded(grad * grad)
    for d in sorted(range(1, 2 * nz), key=lambda d: -min(d // 2, nz - d // 2)):
        there, peer = at_zc(d)
        send(nzc.at[here], nzc.at[here], nzc_s.at[d], nzc_r.at[here], peer)
    for d in range(1, 2 * nz):
        there, peer = at_zc(d)
        copy(nzc.at[here], nzc.at[there], nzc_s.at[d], nzc_r.at[there], peer).wait_recv()
    part = small_square * (1.0 / ny)
    for i in range(2 * nz):
        part = part + nzc[i]
    here = y * nx + x
    nyx[here] = part
    for d in sorted(range(1, ny * nx), key=lambda d: -min(d // nx, ny - d // nx) - min(d % nx, nx - d % nx)):
        there, peer = at_yx(d)
        send(nyx.at[here], nyx.at[here], nyx_s.at[d], nyx_r.at[here], peer)
    for d in range(1, ny * nx):
        there, peer = at_yx(d)
        copy(nyx.at[here], nyx.at[there], nyx_s.at[d], nyx_r.at[there], peer).wait_recv()
    part = nyx[0]
    for i in range(1, ny * nx):
        part = part + nyx[i]
    total = jnp.sum(part, keepdims=True)
    limit = clip_factor * math.sqrt(2 * D * KV_COLS + SMALL_ROWS * D)
    scale = jnp.minimum(1.0, limit / (jnp.sqrt(total) + 1e-06))

    master_new, first_new, second_new = adamw(grad, scale, m1[...], m2[...], mw[...], weight_decay)
    gat[y, c, z] = master_new.astype(BF16)

    def z_block(core, zz, half):
        return gat.at[:, core, zz, half * (LAST_Z // 2) : (half + 1) * (LAST_Z // 2)]

    def piece(core, yy, zz):
        return gat.at[yy, core, zz, LAST_Z:256]

    def half_piece(core, yy, zz, way):
        middle = (LAST_Z + 256) // 2
        return gat.at[yy, core, zz, slice(LAST_Z, middle) if way == 0 else slice(middle, 256)]

    def on_both_y(zz):
        for way in range(2):
            part = piece(c, y, zz)
            send(part, part, b2_s.at[way, zz], b2_r.at[way, zz], at_y(1 if way == 0 else ny - 1)[1])
        send(piece(c, y, zz), piece(c, y, zz), fb_s.at[0, zz], fb_r.at[0, zz], sibling)

    def relay_y(zz):
        for way in range(2):
            sign = 1 if way == 0 else ny - 1
            behind, source = at_y(ny - sign)
            part = piece(c, behind, zz)
            copy(part, part, b2_s.at[way, zz], b2_r.at[way, zz], source).wait_recv()
            half = half_piece(c, behind, zz, way)
            send(half, half, b3_s.at[way, zz], b3_r.at[way, zz], at_y(sign)[1])
            send(part, part, fb_s.at[1 + way, zz], fb_r.at[1 + way, zz], sibling)

    def far_y(zz):
        across, source = at_y(ny // 2)
        for way in range(2):
            half = half_piece(c, across, zz, way)
            copy(half, half, b3_s.at[way, zz], b3_r.at[way, zz], source).wait_recv()
        send(piece(c, across, zz), piece(c, across, zz), fb_s.at[3, zz], fb_r.at[3, zz], sibling)

    b_hops = (nz // 2, nz // 2 - 1)

    def step_b(way, k):
        sign = 1 if way == 0 else nz - 1
        zz = (z + (nz - sign) * k) % nz
        part = piece(c, y, zz)
        if k:
            copy(part, part, b1_s.at[way, k - 1], b1_r.at[way, k - 1], at_z(nz - sign)[1]).wait_recv()
        if k < nz // 2 - 1:
            send(part, part, b1_s.at[way, k], b1_r.at[way, k], at_z(sign)[1])
        if k or way == 0:
            on_both_y(zz)

    def step_g(half, way, k):
        sign = 1 if way == 0 else nz - 1
        zz = (z + (nz - sign) * k) % nz
        part = z_block(c, zz, half)
        if k:
            copy(part, part, gc_s.at[half, way, k - 1], gc_r.at[half, way, k - 1], at_z(nz - sign)[1]).wait_recv()
        if k < z_hops[half, way]:
            send(part, part, gc_s.at[half, way, k], gc_r.at[half, way, k], at_z(sign)[1])
        if k or way == 0:
            send(part, part, fa_s.at[half, way, k], fa_r.at[half, way, k], sibling)

    def around(k):
        return [(z + (nz - k if way == 0 else k)) % nz for way in range(2) if k <= b_hops[way] and (k or way == 0)]

    step_b(0, 0)
    step_b(1, 0)
    part = piece(c, y, z)
    send(part, part, b1_s.at[0, nz // 2 - 1], b1_r.at[0, nz // 2 - 1], at_z(nz // 2)[1])
    for d in range(1, ny):
        yy, peer = at_y(d)
        part = gat.at[y, c, z, 0:LAST_Z]
        send(part, part, a1_s.at[d], a1_r.at[y], peer)

    om[...] = master_new
    o1[...] = first_new
    o2[...] = second_new

    for d in range(1, ny):
        yy, peer = at_y(d)
        part = gat.at[yy, c, z, 0:LAST_Z]
        copy(part, part, a1_s.at[d], a1_r.at[yy], peer).wait_recv()
    for half, way in z_hops:
        step_g(half, way, 0)
    decay = jnp.where(lax.broadcasted_iota(jnp.int32, (SMALL_ROWS, 128), 0) < EXPERTS, weight_decay, 0.0).astype(F32)
    turns = [0, 1, nz // 2, *range(2, nz // 2)]
    for k in range(1, nz // 2 + 1):
        for way in range(2):
            if turns[k] <= b_hops[way]:
                step_b(way, turns[k])
        for zz in around(turns[k - 1]):
            relay_y(zz)
        for half, way in z_hops:
            if k <= z_hops[half, way]:
                step_g(half, way, k)
        for zz in around(turns[k - 2]) if k > 1 else ():
            far_y(zz)
        if k == 1:
            for i in range(nz):
                lanes = slice(i * 128, (i + 1) * 128)
                made = adamw(smf[i, 0:SMALL_ROWS, :], scale, s1[:, lanes], s2[:, lanes], sm[:, lanes], decay)
                osm[:, lanes], os1[:, lanes], os2[:, lanes] = made
                osw[:, lanes] = made[0].astype(BF16)
    for zz in around(turns[-1]):
        relay_y(zz)
    for k in turns[-2:]:
        for zz in around(k):
            far_y(zz)

    for half, way in z_hops:
        for k in range(way, z_hops[half, way] + 1):
            zz = (z + (nz - k if way == 0 else k)) % nz
            copy(z_block(c, zz, half), z_block(other, zz, half), fa_s.at[half, way, k], fa_r.at[half, way, k], sibling).wait_recv()
    for i, d in enumerate((0, ny - 1, 1, ny // 2)):
        yy, _ = at_y(d)
        for zz in range(nz):
            copy(piece(c, yy, zz), piece(other, yy, zz), fb_s.at[i, zz], fb_r.at[i, zz], sibling).wait_recv()
    for made in sent:
        made.wait_send()


def leave(count, *refs):
    semaphores = refs[2 * count]
    copies = [pltpu.make_async_copy(refs[i], refs[count + i], semaphores.at[i]) for i in range(count)]
    for made in copies:
        made.start()
    for made in copies:
        made.wait()


def stored(array):
    rows = array.shape[0]
    return array.reshape(rows, 2, 2, 128).transpose(0, 2, 1, 3).reshape(rows * 4, 128)


def unstored(array):
    rows = array.shape[0] // 4
    return array.reshape(rows, 2, 2, 128).transpose(0, 2, 1, 3).reshape(rows, 2, 256)


def body(
    ny, nx, nz,
    normed_inputs,
    projection_cotangent,
    small_partials,
    master_weights,
    first_moment,
    second_moment,
    small_master,
    small_first,
    small_second,
):
    tokens, features = normed_inputs.shape
    assert ny == 4 and features == ny * 2 * nz * ROWS
    small_shape = jax.ShapeDtypeStruct(small_master.shape, F32)
    owned = jax.ShapeDtypeStruct((4 * ROWS, 128), F32)
    dma = pltpu.SemaphoreType.DMA
    vm = pltpu.VMEM
    last = ROWS - Z_FIRST
    along_y, along_z = [dma((ny,))] * 2, [dma((nz,))] * 2
    pairs, chains = [dma((2,))] * 2, [dma((2, 2, nz // 2))] * 2
    given = (
        normed_inputs, stored(projection_cotangent), small_partials[0],
        stored(master_weights), stored(first_moment), stored(second_moment),
        small_master, small_first, small_second,
    )
    given = [pltpu.with_memory_space_constraint(array, pltpu.HBM) for array in given]
    outs = pl.pallas_call(
        functools.partial(kernel, ny, nx, nz),
        out_shape=(
            owned, owned, owned,
            jax.ShapeDtypeStruct((ny, 2, nz, 4 * ROWS, 128), BF16),
            small_shape, small_shape, small_shape,
            jax.ShapeDtypeStruct(small_master.shape, BF16),
        ),
        in_specs=[pl.BlockSpec(memory_space=pltpu.HBM)] * 9,
        out_specs=[pl.BlockSpec(memory_space=pltpu.VMEM)] * 8,
        scratch_shapes=[
            *[vm(array.shape, array.dtype) for array in given[1:]],
            vm((2 * ny, tokens, nz * ROWS), BF16),
            vm((4 * tokens, 128), F32),
            vm((tokens, 2 * HALF), BF16),
            vm((ny, nz, ROWS, 2 * HALF), BF16),
            vm((ny, nz, ROWS, 2 * HALF), F32),
            vm((ny, nz, ROWS, 2 * HALF), BF16),
            *[vm((2, 2, nz // 2, ny, Z_FIRST, HALF), BF16)] * 2,
            *[vm((2, 2, ny // 2, nz, last, HALF), BF16)] * 2,
            vm((ny, Z_FIRST, 2 * HALF), BF16),
            vm((ny, Z_FIRST, 2 * HALF), F32),
            vm((ny, Z_FIRST, 2 * HALF), BF16),
            *[vm((2, 2, nz // 2, last, HALF), BF16)] * 2,
            vm((nz, last, 2 * HALF), F32),
            vm((4 * ROWS, 128), F32),
            vm((nz, 16, 128), F32),
            vm((nz, 16, 128), F32),
            vm((2, 16, 128), F32),
            vm((ny, 16, 128), F32),
            vm((nz, 16, 128), F32),
            vm((2 * nz, 8, 128), F32),
            vm((ny * nx, 8, 128), F32),
            dma((8,)), dma((2 * ny,)), *along_y, *chains, *[dma((2, 2, ny // 2))] * 2, *along_y, *chains,
            *along_z, *pairs, *along_y, *along_z,
            *[dma((2 * nz,))] * 2, *[dma((ny * nx,))] * 2,
            *along_y, *[dma((2, nz // 2))] * 2, *chains, *[dma((2, nz))] * 4, *[dma((2, 2, nz // 2 + 1))] * 2, *[dma((4, nz))] * 2,
        ],
        compiler_params=pltpu.CompilerParams(
            collective_id=0, has_side_effects=True, vmem_limit_bytes=36 << 20
        ),
    )(*given)
    count = len(outs)
    outs = pl.pallas_call(
        functools.partial(leave, count),
        out_shape=[jax.ShapeDtypeStruct(o.shape, o.dtype) for o in outs],
        in_specs=[pl.BlockSpec(memory_space=pltpu.VMEM)] * count,
        out_specs=[pl.BlockSpec(memory_space=pl.ANY)] * count,
        scratch_shapes=[dma((count,))],
        compiler_params=pltpu.CompilerParams(vmem_limit_bytes=16 << 20),
    )(*outs)
    return (
        unstored(outs[0]), unstored(outs[1]), unstored(outs[2]),
        unstored(outs[3].reshape(-1, 128)),
        outs[4], outs[5], outs[6], outs[7],
    )


def solution(mesh):
    ny, nx, nz = mesh.shape["shard"] // 2, mesh.shape["tensor"], mesh.shape["section"]
    rows = P(("shard", "section"), None, "tensor")
    flat = P(None, "tensor")
    return jax.shard_map(
        functools.partial(body, ny, nx, nz),
        mesh=mesh,
        in_specs=(P(("shard", "section"), None), rows, rows, rows, rows, rows, flat, flat, flat),
        out_specs=(rows, rows, rows, P(None, None, "tensor"), flat, flat, flat, flat),
        check_vma=False,
    )
```
